32 devices in a mesh: rep: 4 (over y, core), tp: 8 (over z, x).
Axes of the slice: x: 2, y: 2, z: 4, core: 2. Of those that a mesh axis runs over, the one named last changes fastest.
Arguments:
- inputs: bfloat16 [16384, 1024], P(('rep', 'tp')), may hold values from -6 to 6
- cotangent: bfloat16 [16384, 8192], P('rep', 'tp'), may hold values from -1 to 1
- master: float32 [1024, 8192], P('rep', 'tp'), may hold values from -6 to 6
- moment: float32 [1024, 8192], P('rep', 'tp'), may hold values from -6 to 6
- second: float32 [1024, 8192], P('rep', 'tp'), may hold values from 0.5 to 4
Outputs:
- combined: float32 [1024, 8192], P('rep', 'tp')
- moment_new: float32 [1024, 8192], P('rep', 'tp')
- second_new: float32 [1024, 8192], P('rep', 'tp')
- master_new: float32 [1024, 8192], P('rep', 'tp')
- weights: bfloat16 [1024, 8192], P(None, 'tp')
The draws below stay inside these ranges and needn't reach their ends.
All inputs are finite; a program needn't handle non-finite values.
Results may differ from the reference program's by a relative error of at most 0.001.
Values may be sent and summed in bfloat16 or wider, within the bound.
A program may use at most 64 MiB of HBM per device.

```python
import math
import jax
import jax.numpy as jnp
from jax import lax

D = 1024
F = 8192
TOK_DEV = 4096
TOKENS = 16384
LEVELS = 2
N_REP = 4


def replica_mix(key, seed_offset):
    replica_count = TOKENS // TOK_DEV
    shared_weight = jax.random.uniform(jax.random.fold_in(key, seed_offset), (replica_count,), jnp.float32, 0.1, 0.95)
    replica_scale = jnp.exp(jax.random.uniform(jax.random.fold_in(key, seed_offset + 1), (replica_count,), jnp.float32, -0.7, 0.7))
    rows_weight = jnp.repeat(shared_weight, TOK_DEV)[:, None]
    rows_scale = jnp.repeat(replica_scale, TOK_DEV)[:, None]
    return (rows_weight, rows_scale)


def mixed_rows(key, width, seed_offset, column_factor):
    rows_weight, rows_scale = replica_mix(key, seed_offset + 5)
    shared = jax.random.normal(jax.random.fold_in(key, seed_offset), (TOK_DEV, width), jnp.float32)
    single = jax.random.normal(jax.random.fold_in(key, seed_offset + 1), (TOKENS, width), jnp.float32)
    mixing = rows_weight * column_factor[None, :]
    rest_weight = jnp.sqrt(1.0 - mixing * mixing)
    tiled = jnp.tile(shared, (TOKENS // TOK_DEV, 1))
    return rows_scale * (mixing * tiled + rest_weight * single)


def draw_inputs(key, part):
    values = mixed_rows(key, D, 11, jnp.ones((D,), jnp.float32))
    return jnp.clip(values, -6.0, 6.0).astype(jnp.bfloat16)


def draw_cotangent(key, part):
    position = jnp.arange(F, dtype=jnp.float32) / F
    column_scale = (0.5 + position) * TOK_DEV ** (-0.5)
    column_factor = 0.1 + 0.9 * position
    values = mixed_rows(key, F, 31, column_factor)
    return jnp.clip(values * column_scale[None, :], -1.0, 1.0).astype(jnp.bfloat16)


def block_levels(rng, dims, cuts, smallest, high):
    def one(axis_at, parts):
        steps = jax.random.uniform(jax.random.fold_in(jax.random.fold_in(rng, 6), axis_at), (parts,), jnp.float32, smallest / len(cuts), high / len(cuts))
        return jnp.repeat(jnp.exp(steps), dims[axis_at] // parts).reshape((-1,) + (1,) * (len(dims) - axis_at - 1))

    level = one(*cuts[0])
    for cut in cuts[1:]:
        level = level * one(*cut)
    return level


def scatter_about(rng, shape, scale, bound, shards=(), kind=jnp.bfloat16):
    drawn = scale * jax.random.normal(rng, shape, jnp.float32)
    if shards:
        drawn = drawn * block_levels(rng, shape, shards, -0.22, 0.18)
    return jnp.clip(drawn, -bound, bound).astype(kind)


def setup_inputs(seed: int = 0) -> dict:
    key_list = jax.random.split(jax.random.key(seed), 6)
    inputs = draw_inputs(jax.random.fold_in(key_list[5], 71), 0)
    cotangent = draw_cotangent(jax.random.fold_in(key_list[5], 71), 0)
    master = scatter_about(key_list[2], (D, F), 1.0, 6.0, ((0, 4), (1, 8)), jnp.float32)
    moment = scatter_about(key_list[3], (D, F), 1.0, 6.0, ((0, 4), (1, 8)), jnp.float32)
    second = jnp.clip(jnp.exp(math.log(4.0) - 2.0794415 * jax.random.uniform(key_list[4], (D, F), jnp.float32) ** block_levels(key_list[4], (D, F), ((0, 4), (1, 8)), -0.2, 0.2)), 0.5, 4.0)
    return dict(inputs=inputs, cotangent=cotangent, master=master, moment=moment, second=second)


EPS_SUM = 1e-06
BETA_ONE = 0.9
BETA_TWO = 0.999
LEARN = 0.01
CORRECT_ONE = 1.0 - 0.9 ** 50
CORRECT_TWO = 1.0 - 0.999 ** 50

def reference(inputs, cotangent, master, moment, second):
    tokens_all = inputs.reshape(N_REP, TOK_DEV, D)
    cotan_all = cotangent.reshape(N_REP, TOK_DEV, F)

    def replica_grad(pair):
        return lax.dot_general(pair[0], pair[1], (((0,), (0,)), ((), ())), preferred_element_type=jnp.float32)
    gradients = lax.map(replica_grad, (tokens_all, cotan_all))
    for level_index in range(LEVELS):
        half_count = gradients.shape[0] // 2
        lower_half = gradients[:half_count]
        upper_half = gradients[half_count:]
        low_low = lax.optimization_barrier(jnp.sum(lower_half * lower_half, axis=(1, 2)))
        high_high = lax.optimization_barrier(jnp.sum(upper_half * upper_half, axis=(1, 2)))
        cross_term = lax.optimization_barrier(jnp.sum(lower_half * upper_half, axis=(1, 2)))
        lower_coef = 1.0 - cross_term / (2.0 * (low_low + EPS_SUM))
        upper_coef = 1.0 - cross_term / (2.0 * (high_high + EPS_SUM))
        gradients = lower_coef[:, None, None] * lower_half + upper_coef[:, None, None] * upper_half
    combined = gradients[0]
    moment_new = BETA_ONE * moment + (1.0 - BETA_ONE) * combined
    second_new = BETA_TWO * second + (1.0 - BETA_TWO) * combined * combined
    master_new = master - LEARN * (moment_new / CORRECT_ONE) / (jnp.sqrt(second_new / CORRECT_TWO) + 1e-08)
    return (combined, moment_new, second_new, master_new, master_new.astype(jnp.bfloat16))
```

```python
import functools
import jax
import jax.numpy as jnp
from jax import lax
from jax.experimental import pallas as pl
from jax.experimental.pallas import tpu as pltpu
from jax.sharding import PartitionSpec as P

EPS_SUM = 1e-06
BETA_ONE = 0.9
BETA_TWO = 0.999
LEARN = 0.01
CORRECT_ONE = 1.0 - 0.9**50
CORRECT_TWO = 1.0 - 0.999**50
LANES = 128
SUBLANES = 8
PIECES = 4
SPLIT = 2
OWN_LEAD = 12
LINE_LEAD = (7, 4.5, 3)
SWAP_LEAD = (10,)
LINE_CROSS = (0.5,)
SWAP_CROSS = (0.5, 5, 3)
SWAPPED = (0, 10, 15)
MESH = pl.DeviceIdType.MESH


def adasum_weights(gram, replicas):
    entries = [{s: jnp.ones((1, 1), jnp.float32)} for s in range(replicas)]

    def inner(left, right):
        total = None
        for i, u in left.items():
            for j, v in right.items():
                term = (u * v) * gram[min(i, j), max(i, j)]
                total = term if total is None else total + term
        return total

    while len(entries) > 1:
        half = len(entries) // 2
        merged = []
        for a, b in zip(entries[:half], entries[half:]):
            aa, bb, ab = inner(a, a), inner(b, b), inner(a, b)
            ca = 1.0 - ab / (2.0 * (aa + EPS_SUM))
            cb = 1.0 - ab / (2.0 * (bb + EPS_SUM))
            merged.append({**{i: ca * u for i, u in a.items()}, **{i: cb * u for i, u in b.items()}})
        entries = merged
    return entries[0]


def timeline(units, outer, inner):
    steps = []
    for k in range(units):
        swap = k in SWAPPED
        n1, n2 = (inner, outer) if swap else (outer, inner)
        steps.append((k - OWN_LEAD, 0, "own", k, 0))
        lead = SWAP_LEAD if swap else LINE_LEAD
        late = k - OWN_LEAD
        for t in range(1, n1):
            late = max(late, k - lead[min(t, len(lead)) - 1])
            steps.append((late, t, "line", k, t))
        lead = SWAP_CROSS if swap else LINE_CROSS
        for u in range(1, n2):
            late = max(late, k - lead[min(u, len(lead)) - 1])
            steps.append((late, n1 + u, "cross", k, u))
        steps.append((max(late, k), n1 + n2, "consume", k, 0))
    return [step[2:] for step in sorted(steps)]


def kernel(
    replicas, outer, inner,
    x_hbm, g_hbm, master_hbm, moment_hbm, second_hbm,
    comb, mom, sec, mas, w_out,
    xg, cot, gsend, gr, master, moment, second, tile_tp, tile_rep,
    load_x, load_g, load_s, x_send, x_recv, g_send, g_recv, t_send, t_recv, r_send, r_recv, w_send, w_recv,
):
    rep = lax.axis_index("rep")
    tp = lax.axis_index("tp")
    peers = outer * inner
    i, j = tp // inner, tp % inner
    units = xg.shape[0] // peers
    tokens, width = xg.shape[1], xg.shape[2]
    chunks = units // SPLIT
    per_segment = chunks // replicas
    segment_order = list(range(replicas - 1, -1, -1))
    rows = gr.shape[1]

    loads = []
    for k in range(units):
        c, part = k // SPLIT, k % SPLIT
        s, h = segment_order[c // per_segment], c % per_segment
        column = pl.multiple_of(((rep ^ s) * per_segment + h) * width, width)
        source = x_hbm.at[pl.ds(part * tokens, tokens), pl.ds(column, width)]
        loads.append(pltpu.make_async_copy(source, xg.at[k * peers + tp], load_x.at[k]))
    for copy in loads:
        copy.start()

    barrier = pltpu.get_barrier_semaphore()
    greeted = replicas - 1
    for ok, to_i, to_j in ((i > 0, i - 1, j), (i + 1 < outer, i + 1, j), (j > 0, i, j - 1), (j + 1 < inner, i, j + 1)):
        target = jnp.clip(to_i, 0, outer - 1) * inner + jnp.clip(to_j, 0, inner - 1)

        @pl.when(ok)
        def _():
            pl.semaphore_signal(barrier, inc=1, device_id=(rep, target), device_id_type=MESH)

        greeted = greeted + jnp.where(ok, 1, 0)
    for s in range(1, replicas):
        pl.semaphore_signal(barrier, inc=1, device_id=(rep ^ s, tp), device_id_type=MESH)

    for part in range(SPLIT):
        for slot in range(peers):
            source = g_hbm.at[pl.ds((slot * SPLIT + part) * tokens, tokens)]
            pltpu.make_async_copy(source, cot.at[part, pl.ds(slot * tokens, tokens)], load_g).start()
    state_loads = [
        pltpu.make_async_copy(src, dst, load_s.at[n])
        for n, (src, dst) in enumerate(((master_hbm, master), (moment_hbm, moment), (second_hbm, second)))
    ]
    for copy in state_loads:
        copy.start()
    pl.semaphore_wait(barrier, greeted)

    def send(k, slot, mark, cond, to_i, to_j):
        target = jnp.clip(to_i, 0, outer - 1) * inner + jnp.clip(to_j, 0, inner - 1)
        block = xg.at[k * peers + slot]

        @pl.when(cond)
        def _():
            pltpu.make_async_remote_copy(
                block, block, x_send.at[k], x_recv.at[k, mark], device_id=(rep, target), device_id_type=MESH
            ).start()

    def wait_blocks(k, mark, count, cond):
        block = xg.at[pl.ds(k * peers, count)]

        @pl.when(cond)
        def _():
            pltpu.make_async_remote_copy(
                block, block, x_send.at[k], x_recv.at[k, mark], device_id=(rep, tp), device_id_type=MESH
            ).wait_recv()

    def route(k):
        if k in SWAPPED:
            return inner, outer, j, i, lambda q1, q2: q2 * inner + q1, lambda q1, q2: (q2, q1)
        return outer, inner, i, j, lambda q1, q2: q1 * inner + q2, lambda q1, q2: (q1, q2)

    def cross(k, slot, cond):
        n1, n2, p1, p2, slot_of, place = route(k)
        send(k, slot, n1 + p2, cond & (p2 + 1 < n2), *place(p1, p2 + 1))
        send(k, slot, n1 + p2, cond & (p2 - 1 >= 0), *place(p1, p2 - 1))

    def own(k):
        n1, n2, p1, p2, slot_of, place = route(k)
        loads[k].wait()
        send(k, tp, p1, p1 + 1 < n1, *place(p1 + 1, p2))
        send(k, tp, p1, p1 - 1 >= 0, *place(p1 - 1, p2))
        cross(k, tp, p1 >= 0)

    def line(k, t):
        n1, n2, p1, p2, slot_of, place = route(k)
        for step in (-1, 1):
            origin = p1 + step * t
            valid = (origin >= 0) & (origin < n1)
            origin = jnp.clip(origin, 0, n1 - 1)
            slot = slot_of(origin, p2)
            wait_blocks(k, origin, 1, valid)
            onward = p1 - step
            send(k, slot, origin, valid & (onward >= 0) & (onward < n1), *place(onward, p2))
            cross(k, slot, valid)

    def second_line(k, u):
        n1, n2, p1, p2, slot_of, place = route(k)
        for step in (-1, 1):
            origin = p2 + step * u
            valid = (origin >= 0) & (origin < n2)
            origin = jnp.clip(origin, 0, n2 - 1)
            wait_blocks(k, n1 + origin, n1, valid)
            onward = p2 - step
            if n2 > 2:
                for r in range(n1):
                    slot = slot_of((p1 + r) % n1, origin)
                    send(k, slot, n1 + origin, valid & (onward >= 0) & (onward < n2), *place(p1, onward))

    def drain(at_i, at_j):
        for k in range(units):
            n1, n2, p1, p2 = (inner, outer, at_j, at_i) if k in SWAPPED else (outer, inner, at_i, at_j)
            count = n1 * ((p2 + 1 < n2) + (p2 > 0))
            count += (1 + p1) * (p1 + 1 < n1) + (n1 - p1) * (p1 > 0)
            count += n1 * (p2 * (p2 + 1 < n2) + (n2 - 1 - p2) * (p2 > 0))
            block = xg.at[pl.ds(0, count)]
            pltpu.make_async_remote_copy(
                block, block, x_send.at[k], x_recv.at[k, 0], device_id=(rep, tp), device_id_type=MESH
            ).wait_send()

    grad_sends = []

    def consume(k):
        c, part = k // SPLIT, k % SPLIT
        s, h = segment_order[c // per_segment], c % per_segment
        at = pl.ds(h * width, width)
        target = gsend.at[s - 1, at] if s else gr.at[0, at]
        product = lax.dot_general(
            xg[pl.ds(k * peers, peers)].reshape(peers * tokens, width), cot[part],
            (((0,), (0,)), ((), ())), preferred_element_type=jnp.float32,
        )
        target[...] = target[...] + product if part else product
        if s and part == SPLIT - 1:
            copy = pltpu.make_async_remote_copy(
                gsend.at[s - 1, at], gr.at[s, at], g_send.at[s - 1, h], g_recv.at[s - 1, h],
                device_id=(rep ^ s, tp), device_id_type=MESH,
            )
            copy.start()
            grad_sends.append((h, copy))

    pairs = [(s, t) for s in range(replicas) for t in range(s, replicas)]
    fold = gr.shape[2] // LANES

    def inner_products(h, sums):
        for at_h, copy in grad_sends:
            if at_h == h:
                copy.wait_recv()

        def products(n, sums):
            at = pl.ds(pl.multiple_of(h * width + n * SUBLANES, SUBLANES), SUBLANES)
            block = [gr[s, at, :] for s in range(replicas)]
            out = []
            for total, (s, t) in zip(sums, pairs):
                prod = block[s] * block[t]
                part = prod[:, :LANES]
                for f in range(1, fold):
                    part = part + prod[:, f * LANES : (f + 1) * LANES]
                out.append(total + part)
            return tuple(out)

        return lax.fori_loop(0, width // SUBLANES, products, sums)

    sums = tuple(jnp.zeros((SUBLANES, LANES), jnp.float32) for _ in pairs)
    loaded = False
    for kind, k, t in timeline(units, outer, inner):
        if kind == "own":
            own(k)
        elif kind == "line":
            line(k, t)
        elif kind == "cross":
            second_line(k, t)
        else:
            if not loaded:
                pltpu.make_async_copy(cot, cot, load_g).wait()
                loaded = True
            consume(k)
            if k == units - SPLIT - 1:
                for h in range(per_segment - 1):
                    sums = inner_products(h, sums)
    sums = inner_products(per_segment - 1, sums)
    seg_sends = [copy for _, copy in grad_sends]
    lane = lax.broadcasted_iota(jnp.int32, (SUBLANES, LANES), 1)
    packed = jnp.zeros((SUBLANES, LANES), jnp.float32)
    for n, total in enumerate(sums):
        packed = jnp.where(lane == n, jnp.sum(total, axis=1, keepdims=True), packed)
    tile_tp[0] = packed
    tile_sends = []
    for d in range(1, peers):
        copy = pltpu.make_async_remote_copy(
            tile_tp.at[0], tile_tp.at[d], t_send.at[d - 1], t_recv.at[d - 1],
            device_id=(rep, (tp + d) % peers), device_id_type=MESH,
        )
        copy.start()
        tile_sends.append(copy)
    for copy in state_loads:
        copy.wait()
    for copy in tile_sends:
        copy.wait_recv()
    packed = tile_tp[0]
    for d in range(1, peers):
        packed = packed + tile_tp[d]
    tile_rep[0] = packed
    for s in range(1, replicas):
        copy = pltpu.make_async_remote_copy(
            tile_rep.at[0], tile_rep.at[s], r_send.at[s - 1], r_recv.at[s - 1],
            device_id=(rep ^ s, tp), device_id_type=MESH,
        )
        copy.start()
        tile_sends.append(copy)
    for copy in tile_sends[peers - 1 :]:
        copy.wait_recv()
    index = {pair: n for n, pair in enumerate(pairs)}
    seen = [tile_rep[s] for s in range(replicas)]
    gram = {}
    for s, t in pairs:
        value = None
        for d in range(replicas):
            p, q = s ^ d, t ^ d
            picked = jnp.where(lane == index[min(p, q), max(p, q)], seen[d], 0.0)
            value = picked if value is None else value + picked
        gram[s, t] = jnp.sum(value, keepdims=True)
    coef = adasum_weights(gram, replicas)
    coef = [jnp.broadcast_to(coef[s], (SUBLANES, gr.shape[2])) for s in range(replicas)]

    masks = []
    mask = replicas // 2
    while mask:
        masks.append(mask)
        mask //= 2
    piece = rows // PIECES
    w_copies = {}

    def w_at(s, q):
        return w_out.at[pl.ds(pl.multiple_of((rep ^ s) * rows + q * piece, piece), piece)]

    def w_send_start(step, s, q):
        m = masks[step]
        copy = pltpu.make_async_remote_copy(
            w_at(s, q), w_at(s, q), w_send.at[s ^ m, q], w_recv.at[s ^ m, q],
            device_id=(rep ^ m, tp), device_id_type=MESH,
        )
        copy.start()
        w_copies[s ^ m, q] = copy

    for q in range(PIECES):
        def update(n, carry):
            at = pl.ds(pl.multiple_of(q * piece + n * SUBLANES * 2, SUBLANES * 2), SUBLANES * 2)
            value = None
            for s in range(replicas):
                term = coef[s][:1] * gr[s, at, :]
                value = term if value is None else value + term
            moment_new = BETA_ONE * moment[at, :] + (1.0 - BETA_ONE) * value
            second_new = BETA_TWO * second[at, :] + (1.0 - BETA_TWO) * value * value
            master_new = master[at, :] - LEARN * (moment_new / CORRECT_ONE) / (
                jnp.sqrt(second_new / CORRECT_TWO) + 1e-08
            )
            comb[at, :] = value
            mom[at, :] = moment_new
            sec[at, :] = second_new
            mas[at, :] = master_new
            own_at = pl.ds(pl.multiple_of(rep * rows + q * piece + n * SUBLANES * 2, SUBLANES * 2), SUBLANES * 2)
            w_out[own_at, :] = master_new.astype(jnp.bfloat16)
            return carry

        lax.fori_loop(0, piece // (SUBLANES * 2), update, 0)
        for step in range(len(masks)):
            w_send_start(step, 0, q)
    def relay(q, step, s):
        w_copies[s, q].wait_recv()
        for later in range(step + 1, len(masks)):
            w_send_start(later, s, q)

    held = [0]
    for step, m in enumerate(masks):
        fresh = [s ^ m for s in held]
        for q in range(PIECES):
            for s in fresh:
                relay(q, step, s)
        held = held + fresh

    for at_i in range(outer):
        for at_j in range(inner):
            pl.when((i == at_i) & (j == at_j))(functools.partial(drain, at_i, at_j))
    for copy in seg_sends + tile_sends + list(w_copies.values()):
        copy.wait_send()


def deliver(*refs):
    sources, targets, sem = refs[:5], refs[5:10], refs[10]
    moves = []
    for n, (src, dst) in enumerate(zip(sources, targets)):
        step = src.shape[0] // PIECES
        for q in range(PIECES):
            at = pl.ds(q * step, step)
            moves.append(pltpu.make_async_copy(src.at[at], dst.at[at], sem.at[n, q]))
            moves[-1].start()
    for move in moves:
        move.wait()


def per_device(inputs, cotangent, master, moment, second):
    replicas = lax.axis_size("rep")
    peers = lax.axis_size("tp")
    inner = 1 << (peers.bit_length() - 1) // 2
    outer = peers // inner
    tokens, depth = inputs.shape
    features = cotangent.shape[1]
    rows = depth // replicas
    width = min(LANES, rows)
    chunks = depth // width
    per_segment = rows // width
    units = chunks * SPLIT
    anywhere = pl.BlockSpec(memory_space=pl.ANY)
    vmem = pl.BlockSpec(memory_space=pltpu.VMEM)
    dma = pltpu.SemaphoreType.DMA
    small = pltpu.VMEM((rows, features), jnp.float32)
    results = pl.pallas_call(
        functools.partial(kernel, replicas, outer, inner),
        out_shape=(small, small, small, small, pltpu.VMEM((depth, features), jnp.bfloat16)),
        in_specs=[anywhere] * 5,
        out_specs=(vmem,) * 5,
        scratch_shapes=[
            pltpu.VMEM((units * peers, tokens // SPLIT, width), jnp.bfloat16),
            pltpu.VMEM((SPLIT, cotangent.shape[0] // SPLIT, features), jnp.bfloat16),
            pltpu.VMEM((replicas - 1, rows, features), jnp.float32),
            pltpu.VMEM((replicas, rows, features), jnp.float32),
            small, small, small,
            pltpu.VMEM((peers, SUBLANES, LANES), jnp.float32),
            pltpu.VMEM((replicas, SUBLANES, LANES), jnp.float32),
            dma((units,)),
            dma(()),
            dma((3,)),
            dma((units,)),
            dma((units, outer + inner)),
            dma((replicas - 1, per_segment)),
            dma((replicas - 1, per_segment)),
            dma((peers - 1,)),
            dma((peers - 1,)),
            dma((replicas - 1,)),
            dma((replicas - 1,)),
            dma((replicas, PIECES)),
            dma((replicas, PIECES)),
        ],
        compiler_params=pltpu.CompilerParams(
            collective_id=0, has_side_effects=True, vmem_limit_bytes=48 * 1024 * 1024
        ),
        name="adasum_adam",
    )(inputs, cotangent, master, moment, second)
    results = [pltpu.with_memory_space_constraint(r, pltpu.VMEM) for r in results]
    return pl.pallas_call(
        deliver,
        out_shape=tuple(jax.ShapeDtypeStruct(r.shape, r.dtype) for r in results),
        in_specs=[vmem] * 5,
        out_specs=(anywhere,) * 5,
        scratch_shapes=[dma((5, PIECES))],
        compiler_params=pltpu.CompilerParams(vmem_limit_bytes=1024 * 1024),
        name="deliver",
    )(*results)


def solution(mesh):
    return jax.shard_map(
        per_device,
        mesh=mesh,
        in_specs=(
            P(("rep", "tp"), None),
            P("rep", "tp"),
            P("rep", "tp"),
            P("rep", "tp"),
            P("rep", "tp"),
        ),
        out_specs=(P("rep", "tp"), P("rep", "tp"), P("rep", "tp"), P("rep", "tp"), P(None, "tp")),
        check_vma=False,
    )
```

```python
import functools
import jax
import jax.numpy as jnp
from jax import lax
from jax.experimental import pallas as pl
from jax.experimental.pallas import tpu as pltpu
from jax.sharding import PartitionSpec as P

EPS_SUM = 1e-06
BETA_ONE = 0.9
BETA_TWO = 0.999
LEARN = 0.01
CORRECT_ONE = 1.0 - 0.9**50
CORRECT_TWO = 1.0 - 0.999**50
LANES = 128
SUBLANES = 8
PIECES = 4
SPLIT = 2
OWN_LEAD = 11
LINE_LEAD = (7, 5.5, 3.5)
SWAP_LEAD = (6.5,)
LINE_CROSS = (0,)
SWAP_CROSS = (3.5, 2.5, 0)
SWAPPED = (8, 12, 15)
GROUP = 4
BATCH = 8
MESH = pl.DeviceIdType.MESH


def adasum_weights(gram, replicas):
    entries = [{s: jnp.ones((1, 1), jnp.float32)} for s in range(replicas)]

    def inner(left, right):
        total = None
        for i, u in left.items():
            for j, v in right.items():
                term = (u * v) * gram[min(i, j), max(i, j)]
                total = term if total is None else total + term
        return total

    while len(entries) > 1:
        half = len(entries) // 2
        merged = []
        for a, b in zip(entries[:half], entries[half:]):
            aa, bb, ab = inner(a, a), inner(b, b), inner(a, b)
            ca = 1.0 - ab / (2.0 * (aa + EPS_SUM))
            cb = 1.0 - ab / (2.0 * (bb + EPS_SUM))
            merged.append({**{i: ca * u for i, u in a.items()}, **{i: cb * u for i, u in b.items()}})
        entries = merged
    return entries[0]


def timeline(units, outer, inner):
    steps = []
    for k in range(units):
        swap = k in SWAPPED
        n1, n2 = (inner, outer) if swap else (outer, inner)
        steps.append((k - OWN_LEAD, 0, "own", k, 0))
        lead = SWAP_LEAD if swap else LINE_LEAD
        late = k - OWN_LEAD
        for t in range(1, n1):
            late = max(late, k - lead[min(t, len(lead)) - 1])
            steps.append((late, t, "line", k, t))
        lead = SWAP_CROSS if swap else LINE_CROSS
        for u in range(1, n2):
            late = max(late, k - lead[min(u, len(lead)) - 1])
            steps.append((late, n1 + u, "cross", k, u))
        steps.append((max(late, k), n1 + n2, "consume", k, 0))
    return [step[2:] for step in sorted(steps)]


def kernel(
    replicas, outer, inner,
    x_hbm, g_hbm, master_hbm, moment_hbm, second_hbm,
    comb, mom, sec, mas, w_out,
    xg, cot, gsend, gr, states, tile_tp,
    load_x, load_g, load_s, x_send, x_recv, g_send, g_recv, t_send, t_recv, w_send, w_recv, w_last,
):
    rep = lax.axis_index("rep")
    tp = lax.axis_index("tp")
    peers = outer * inner
    i, j = tp // inner, tp % inner
    units = xg.shape[0] // peers
    tokens, width = xg.shape[1], xg.shape[2]
    chunks = units // SPLIT
    per_segment = chunks // replicas
    segment_order = list(range(replicas - 1, -1, -1))
    rows = gr.shape[1]

    for k in range(units):
        c, part = k // SPLIT, k % SPLIT
        s, h = segment_order[c // per_segment], c % per_segment
        column = pl.multiple_of(((rep ^ s) * per_segment + h) * width, width)
        source = x_hbm.at[pl.ds(part * tokens, tokens), pl.ds(column, width)]
        pltpu.make_async_copy(source, xg.at[k * peers + tp], load_x.at[k // GROUP]).start()

    barrier = pltpu.get_barrier_semaphore()
    greeted = replicas - 1
    for ok, to_i, to_j in ((i > 0, i - 1, j), (i + 1 < outer, i + 1, j), (j > 0, i, j - 1), (j + 1 < inner, i, j + 1)):
        target = jnp.clip(to_i, 0, outer - 1) * inner + jnp.clip(to_j, 0, inner - 1)

        @pl.when(ok)
        def _():
            pl.semaphore_signal(barrier, inc=1, device_id=(rep, target), device_id_type=MESH)

        greeted = greeted + jnp.where(ok, 1, 0)
    for s in range(1, replicas):
        pl.semaphore_signal(barrier, inc=1, device_id=(rep ^ s, tp), device_id_type=MESH)

    for part in range(SPLIT):
        for slot in range(peers):
            source = g_hbm.at[pl.ds((slot * SPLIT + part) * tokens, tokens)]
            pltpu.make_async_copy(source, cot.at[part, pl.ds(slot * tokens, tokens)], load_g).start()
    for n, source in enumerate((master_hbm, moment_hbm, second_hbm)):
        pltpu.make_async_copy(source, states.at[n], load_s).start()
    pl.semaphore_wait(barrier, greeted)

    def send(k, slot, mark, cond, to_i, to_j):
        target = jnp.clip(to_i, 0, outer - 1) * inner + jnp.clip(to_j, 0, inner - 1)
        block = xg.at[k * peers + slot]

        @pl.when(cond)
        def _():
            pltpu.make_async_remote_copy(
                block, block, x_send.at[k // BATCH], x_recv.at[k, mark], device_id=(rep, target), device_id_type=MESH
            ).start()

    def wait_blocks(k, mark, count, cond):
        block = xg.at[pl.ds(k * peers, count)]

        @pl.when(cond)
        def _():
            pltpu.make_async_remote_copy(
                block, block, x_send.at[0], x_recv.at[k, mark], device_id=(rep, tp), device_id_type=MESH
            ).wait_recv()

    def route(k):
        if k in SWAPPED:
            return inner, outer, j, i, lambda q1, q2: q2 * inner + q1, lambda q1, q2: (q2, q1)
        return outer, inner, i, j, lambda q1, q2: q1 * inner + q2, lambda q1, q2: (q1, q2)

    def cross(k, slot, cond):
        n1, n2, p1, p2, slot_of, place = route(k)
        send(k, slot, n1 - 1 + p2, cond & (p2 + 1 < n2), *place(p1, p2 + 1))
        send(k, slot, n1 - 2 + p2, cond & (p2 - 1 >= 0), *place(p1, p2 - 1))

    def own(k):
        n1, n2, p1, p2, slot_of, place = route(k)
        if k % GROUP == 0:
            block = xg.at[pl.ds(0, min(GROUP, units - k))]
            pltpu.make_async_copy(block, block, load_x.at[k // GROUP]).wait()
        send(k, tp, p1, p1 + 1 < n1, *place(p1 + 1, p2))
        send(k, tp, p1 - 1, p1 - 1 >= 0, *place(p1 - 1, p2))
        cross(k, tp, p1 >= 0)

    def line(k, t):
        n1, n2, p1, p2, slot_of, place = route(k)
        for step in (-1, 1):
            origin = p1 + step * t
            valid = (origin >= 0) & (origin < n1)
            origin = jnp.clip(origin, 0, n1 - 1)
            slot = slot_of(origin, p2)
            mark = jnp.clip(origin - (step > 0), 0, n1 - 2)
            wait_blocks(k, mark, 1, valid)
            onward = p1 - step
            send(k, slot, mark, valid & (onward >= 0) & (onward < n1), *place(onward, p2))
            cross(k, slot, valid)

    def second_line(k, u):
        n1, n2, p1, p2, slot_of, place = route(k)
        for step in (-1, 1):
            origin = p2 + step * u
            valid = (origin >= 0) & (origin < n2)
            origin = jnp.clip(origin, 0, n2 - 1)
            mark = n1 - 1 + jnp.clip(origin - (step > 0), 0, n2 - 2)
            wait_blocks(k, mark, n1, valid)
            onward = p2 - step
            if n2 > 2:
                for r in range(n1):
                    slot = slot_of((p1 + r) % n1, origin)
                    send(k, slot, mark, valid & (onward >= 0) & (onward < n2), *place(p1, onward))

    def drain(at_i, at_j):
        totals = [0] * -(-units // BATCH)
        for k in range(units):
            n1, n2, p1, p2 = (inner, outer, at_j, at_i) if k in SWAPPED else (outer, inner, at_i, at_j)
            count = n1 * ((p2 + 1 < n2) + (p2 > 0))
            count += (1 + p1) * (p1 + 1 < n1) + (n1 - p1) * (p1 > 0)
            count += n1 * (p2 * (p2 + 1 < n2) + (n2 - 1 - p2) * (p2 > 0))
            totals[k // BATCH] += count
        for n, count in enumerate(totals):
            block = xg.at[pl.ds(0, count)]
            pltpu.make_async_remote_copy(
                block, block, x_send.at[n], x_recv.at[0, 0], device_id=(rep, tp), device_id_type=MESH
            ).wait_send()

    def consume(k):
        c, part = k // SPLIT, k % SPLIT
        s, h = segment_order[c // per_segment], c % per_segment
        at = pl.ds(h * width, width)
        target = gsend.at[s - 1, at] if s else gr.at[0, at]
        product = lax.dot_general(
            xg[pl.ds(k * peers, peers)].reshape(peers * tokens, width), cot[part],
            (((0,), (0,)), ((), ())), preferred_element_type=jnp.float32,
        )
        target[...] = target[...] + product if part else product
        if s and part == SPLIT - 1:
            copy = pltpu.make_async_remote_copy(
                gsend.at[s - 1, at], gr.at[s, at], g_send, g_recv.at[h],
                device_id=(rep ^ s, tp), device_id_type=MESH,
            )
            copy.start()

    pairs = [(s, t) for s in range(replicas) for t in range(s, replicas)]
    fold = gr.shape[2] // LANES

    def inner_products(h, sums):
        piece = gr.at[pl.ds(0, replicas - 1), pl.ds(h * width, width)]
        pltpu.make_async_copy(piece, piece, g_recv.at[h]).wait()

        def products(n, sums):
            at = pl.ds(pl.multiple_of(h * width + n * SUBLANES, SUBLANES), SUBLANES)
            block = [gr[s, at, :] for s in range(replicas)]
            out = []
            for total, (s, t) in zip(sums, pairs):
                prod = block[s] * block[t]
                part = prod[:, :LANES]
                for f in range(1, fold):
                    part = part + prod[:, f * LANES : (f + 1) * LANES]
                out.append(total + part)
            return tuple(out)

        return lax.fori_loop(0, width // SUBLANES, products, sums)

    sums = tuple(jnp.zeros((SUBLANES, LANES), jnp.float32) for _ in pairs)
    loaded = False
    for kind, k, t in timeline(units, outer, inner):
        if kind == "own":
            own(k)
        elif kind == "line":
            line(k, t)
        elif kind == "cross":
            second_line(k, t)
        else:
            if not loaded:
                pltpu.make_async_copy(cot, cot, load_g).wait()
                loaded = True
            consume(k)
            if k == units - 2:
                for h in range(per_segment - 1):
                    sums = inner_products(h, sums)
    sums = inner_products(per_segment - 1, sums)
    lane = lax.broadcasted_iota(jnp.int32, (SUBLANES, LANES), 1)
    packed = jnp.zeros((SUBLANES, LANES), jnp.float32)
    for n, total in enumerate(sums):
        packed = jnp.where(lane == n, jnp.sum(total, axis=1, keepdims=True), packed)
    tile_tp[0] = packed
    for d in range(peers - 1, -1, -1):
        for s in range(replicas - 1, -1, -1):
            if d or s:
                pltpu.make_async_remote_copy(
                    tile_tp.at[0], tile_tp.at[s * peers + d], t_send, t_recv,
                    device_id=(rep ^ s, (tp + d) % peers), device_id_type=MESH,
                ).start()
    pltpu.make_async_copy(states, states, load_s).wait()
    others = tile_tp.at[pl.ds(1, replicas * peers - 1)]
    pltpu.make_async_copy(others, others, t_recv).wait()
    index = {pair: n for n, pair in enumerate(pairs)}
    seen = []
    for s in range(replicas):
        total = tile_tp[s * peers]
        for d in range(1, peers):
            total = total + tile_tp[s * peers + d]
        seen.append(total)
    gram = {}
    for s, t in pairs:
        value = None
        for d in range(replicas):
            p, q = s ^ d, t ^ d
            picked = jnp.where(lane == index[min(p, q), max(p, q)], seen[d], 0.0)
            value = picked if value is None else value + picked
        gram[s, t] = jnp.sum(value, keepdims=True)
    coef = adasum_weights(gram, replicas)
    coef = [jnp.broadcast_to(coef[s], (SUBLANES, gr.shape[2])) for s in range(replicas)]

    masks = []
    mask = replicas // 2
    while mask:
        masks.append(mask)
        mask //= 2
    piece = rows // PIECES

    def w_at(s, q):
        return w_out.at[pl.ds(pl.multiple_of((rep ^ s) * rows + q * piece, piece), piece)]

    last = len(masks) - 1

    def w_send_start(step, s, q):
        m = masks[step]
        pltpu.make_async_remote_copy(
            w_at(s, q), w_at(s, q), w_send, w_last if step == last else w_recv.at[s ^ m, q],
            device_id=(rep ^ m, tp), device_id_type=MESH,
        ).start()

    for q in range(PIECES):
        def update(n, carry):
            at = pl.ds(pl.multiple_of(q * piece + n * SUBLANES * 2, SUBLANES * 2), SUBLANES * 2)
            value = None
            for s in range(replicas):
                term = coef[s][:1] * gr[s, at, :]
                value = term if value is None else value + term
            moment_new = BETA_ONE * states[1, at, :] + (1.0 - BETA_ONE) * value
            second_new = BETA_TWO * states[2, at, :] + (1.0 - BETA_TWO) * value * value
            master_new = states[0, at, :] - LEARN * (moment_new / CORRECT_ONE) / (
                jnp.sqrt(second_new / CORRECT_TWO) + 1e-08
            )
            comb[at, :] = value
            mom[at, :] = moment_new
            sec[at, :] = second_new
            mas[at, :] = master_new
            own_at = pl.ds(pl.multiple_of(rep * rows + q * piece + n * SUBLANES * 2, SUBLANES * 2), SUBLANES * 2)
            w_out[own_at, :] = master_new.astype(jnp.bfloat16)
            return carry

        lax.fori_loop(0, piece // (SUBLANES * 2), update, 0)
        for step in range(len(masks)):
            w_send_start(step, 0, q)
    def relay(q, step, s):
        pltpu.make_async_copy(w_at(s, q), w_at(s, q), w_recv.at[s, q]).wait()
        for later in range(step + 1, len(masks)):
            w_send_start(later, s, q)

    held = [0]
    for step, m in enumerate(masks[:-1]):
        fresh = [s ^ m for s in held]
        for q in range(PIECES):
            for s in fresh:
                relay(q, step, s)
        held = held + fresh

    half = w_out.at[pl.ds(0, replicas // 2 * rows)]
    pltpu.make_async_copy(half, half, w_last).wait()
    for at_i in range(outer):
        for at_j in range(inner):
            pl.when((i == at_i) & (j == at_j))(functools.partial(drain, at_i, at_j))
    pltpu.make_async_copy(gsend, gsend, g_send).wait()
    pltpu.make_async_copy(others, others, t_send).wait()
    sent = w_out.at[pl.ds(0, (replicas - 1) * rows)]
    pltpu.make_async_copy(sent, sent, w_send).wait()


def deliver(*refs):
    sources, targets, sem = refs[:5], refs[5:10], refs[10]
    moves = []
    for n, (src, dst) in enumerate(zip(sources, targets)):
        step = src.shape[0] // PIECES
        for q in range(PIECES):
            at = pl.ds(q * step, step)
            moves.append(pltpu.make_async_copy(src.at[at], dst.at[at], sem.at[n, q]))
            moves[-1].start()
    for move in moves:
        move.wait()


def per_device(inputs, cotangent, master, moment, second):
    replicas = lax.axis_size("rep")
    peers = lax.axis_size("tp")
    inner = 1 << (peers.bit_length() - 1) // 2
    outer = peers // inner
    tokens, depth = inputs.shape
    features = cotangent.shape[1]
    rows = depth // replicas
    width = min(LANES, rows)
    chunks = depth // width
    per_segment = rows // width
    units = chunks * SPLIT
    anywhere = pl.BlockSpec(memory_space=pl.ANY)
    vmem = pl.BlockSpec(memory_space=pltpu.VMEM)
    dma = pltpu.SemaphoreType.DMA
    small = pltpu.VMEM((rows, features), jnp.float32)
    results = pl.pallas_call(
        functools.partial(kernel, replicas, outer, inner),
        out_shape=(small, small, small, small, pltpu.VMEM((depth, features), jnp.bfloat16)),
        in_specs=[anywhere] * 5,
        out_specs=(vmem,) * 5,
        scratch_shapes=[
            pltpu.VMEM((units * peers, tokens // SPLIT, width), jnp.bfloat16),
            pltpu.VMEM((SPLIT, cotangent.shape[0] // SPLIT, features), jnp.bfloat16),
            pltpu.VMEM((replicas - 1, rows, features), jnp.float32),
            pltpu.VMEM((replicas, rows, features), jnp.float32),
            pltpu.VMEM((3, rows, features), jnp.float32),
            pltpu.VMEM((replicas * peers, SUBLANES, LANES), jnp.float32),
            dma((-(-units // GROUP),)),
            dma(()),
            dma(()),
            dma((-(-units // BATCH),)),
            dma((units, outer + inner - 2)),
            dma(()),
            dma((per_segment,)),
            dma(()),
            dma(()),
            dma(()),
            dma((replicas, PIECES)),
            dma(()),
        ],
        compiler_params=pltpu.CompilerParams(
            collective_id=0, has_side_effects=True, vmem_limit_bytes=48 * 1024 * 1024
        ),
        name="adasum_adam",
    )(inputs, cotangent, master, moment, second)
    results = [pltpu.with_memory_space_constraint(r, pltpu.VMEM) for r in results]
    return pl.pallas_call(
        deliver,
        out_shape=tuple(jax.ShapeDtypeStruct(r.shape, r.dtype) for r in results),
        in_specs=[vmem] * 5,
        out_specs=(anywhere,) * 5,
        scratch_shapes=[dma((5, PIECES))],
        compiler_params=pltpu.CompilerParams(vmem_limit_bytes=1024 * 1024),
        name="deliver",
    )(*results)


def solution(mesh):
    return jax.shard_map(
        per_device,
        mesh=mesh,
        in_specs=(
            P(("rep", "tp"), None),
            P("rep", "tp"),
            P("rep", "tp"),
            P("rep", "tp"),
            P("rep", "tp"),
        ),
        out_specs=(P("rep", "tp"), P("rep", "tp"), P("rep", "tp"), P("rep", "tp"), P(None, "tp")),
        check_vma=False,
    )
```

```python
import functools
import jax
import jax.numpy as jnp
from jax import lax
from jax.experimental import pallas as pl
from jax.experimental.pallas import tpu as pltpu
from jax.sharding import PartitionSpec as P

EPS_SUM = 1e-06
BETA_ONE = 0.9
BETA_TWO = 0.999
LEARN = 0.01
CORRECT_ONE = 1.0 - 0.9**50
CORRECT_TWO = 1.0 - 0.999**50
LANES = 128
SUBLANES = 8
PIECES = 8
SPLIT = 2
OWN_LEAD = 9
LINE_LEAD = (4.5, 3.5, 2.5)
SWAP_LEAD = (7.0,)
LINE_CROSS = (0,)
SWAP_CROSS = (4.0, 2.0, 1.5)
SWAPPED = (5, 14)
GROUP = 4
BATCH = 8
MIXED = 11
MESH = pl.DeviceIdType.MESH


def adasum_weights(gram, replicas):
    entries = [{s: jnp.ones((1, 1), jnp.float32)} for s in range(replicas)]

    def inner(left, right):
        total = None
        for i, u in left.items():
            for j, v in right.items():
                term = (u * v) * gram[min(i, j), max(i, j)]
                total = term if total is None else total + term
        return total

    while len(entries) > 1:
        half = len(entries) // 2
        merged = []
        for a, b in zip(entries[:half], entries[half:]):
            aa, bb, ab = inner(a, a), inner(b, b), inner(a, b)
            ca = 1.0 - ab / (2.0 * (aa + EPS_SUM))
            cb = 1.0 - ab / (2.0 * (bb + EPS_SUM))
            merged.append({**{i: ca * u for i, u in a.items()}, **{i: cb * u for i, u in b.items()}})
        entries = merged
    return entries[0]


def timeline(units, outer, inner):
    steps = []
    for k in range(units):
        mixed = k == MIXED and inner == 2
        swap = not mixed and k in SWAPPED + (MIXED,)
        n1, n2 = (inner, outer) if swap else (outer, inner)
        steps.append((k - OWN_LEAD, 0, "own", k, 0))
        lead = SWAP_LEAD if swap else LINE_LEAD
        late = k - OWN_LEAD
        for t in range(1, n1):
            late = max(late, k - lead[min(t, len(lead)) - 1])
            steps.append((late, t, "line", k, t))
        if mixed:
            turn = max(k - OWN_LEAD, k - SWAP_LEAD[0])
            steps.append((turn, 0.5, "turn", k, 0))
            for u in range(1, n1):
                turn = max(turn, k - SWAP_CROSS[min(u, len(SWAP_CROSS)) - 1])
                steps.append((turn, n1 + u, "pass", k, u))
        lead = SWAP_CROSS if swap else LINE_CROSS
        for u in range(1, n2):
            late = max(late, k - lead[min(u, len(lead)) - 1])
            steps.append((late, n1 + u, "cross", k, u))
        steps.append((max(late, k), n1 + n2, "consume", k, 0))
    return [step[2:] for step in sorted(steps)]


def kernel(
    replicas, outer, inner,
    x_hbm, g_hbm, master_hbm, moment_hbm, second_hbm,
    comb, mom, sec, mas, w_out,
    xg, cot, gsend, gr, states, tile_tp,
    load_x, load_g, load_s, x_send, x_recv, m_recv, g_send, g_recv, t_send, t_recv, w_send, w_recv, w_last,
):
    rep = lax.axis_index("rep")
    tp = lax.axis_index("tp")
    peers = outer * inner
    i, j = tp // inner, tp % inner
    units = xg.shape[0] // peers
    tokens, width = xg.shape[1], xg.shape[2]
    swapped = SWAPPED if inner == 2 else SWAPPED + (MIXED,)
    mixed = MIXED if inner == 2 else units
    middle = (outer // 2 - 1, outer // 2)
    chunks = units // SPLIT
    per_segment = chunks // replicas
    segment_order = list(range(replicas - 1, -1, -1))
    rows = gr.shape[1]

    for k in range(units):
        c, part = k // SPLIT, k % SPLIT
        s, h = segment_order[c // per_segment], c % per_segment
        column = pl.multiple_of(((rep ^ s) * per_segment + h) * width, width)
        source = x_hbm.at[pl.ds(part * tokens, tokens), pl.ds(column, width)]
        pltpu.make_async_copy(source, xg.at[k * peers + tp], load_x.at[k // GROUP]).start()

    barrier = pltpu.get_barrier_semaphore()
    greeted = replicas - 1
    for ok, to_i, to_j in ((i > 0, i - 1, j), (i + 1 < outer, i + 1, j), (j > 0, i, j - 1), (j + 1 < inner, i, j + 1)):
        target = jnp.clip(to_i, 0, outer - 1) * inner + jnp.clip(to_j, 0, inner - 1)

        @pl.when(ok)
        def _():
            pl.semaphore_signal(barrier, inc=1, device_id=(rep, target), device_id_type=MESH)

        greeted = greeted + jnp.where(ok, 1, 0)
    for s in range(1, replicas):
        pl.semaphore_signal(barrier, inc=1, device_id=(rep ^ s, tp), device_id_type=MESH)

    for part in range(SPLIT):
        for slot in range(peers):
            source = g_hbm.at[pl.ds((slot * SPLIT + part) * tokens, tokens)]
            pltpu.make_async_copy(source, cot.at[part, pl.ds(slot * tokens, tokens)], load_g).start()
    for n, source in enumerate((master_hbm, moment_hbm, second_hbm)):
        pltpu.make_async_copy(source, states.at[n], load_s).start()
    pl.semaphore_wait(barrier, greeted)

    def send(k, slot, mark, cond, to_i, to_j, arrived=None):
        target = jnp.clip(to_i, 0, outer - 1) * inner + jnp.clip(to_j, 0, inner - 1)
        block = xg.at[k * peers + slot]

        @pl.when(cond)
        def _():
            pltpu.make_async_remote_copy(
                block, block, x_send.at[k // BATCH], x_recv.at[k, mark] if arrived is None else arrived, device_id=(rep, target), device_id_type=MESH
            ).start()

    def wait_blocks(k, mark, count, cond, arrived=None):
        block = xg.at[pl.ds(k * peers, count)]

        @pl.when(cond)
        def _():
            pltpu.make_async_remote_copy(
                block, block, x_send.at[0], x_recv.at[k, mark] if arrived is None else arrived, device_id=(rep, tp), device_id_type=MESH
            ).wait_recv()

    def route(k):
        if k in swapped:
            return inner, outer, j, i, lambda q1, q2: q2 * inner + q1, lambda q1, q2: (q2, q1)
        return outer, inner, i, j, lambda q1, q2: q1 * inner + q2, lambda q1, q2: (q1, q2)

    def cross(k, slot, cond):
        n1, n2, p1, p2, slot_of, place = route(k)
        send(k, slot, n1 - 1 + p2, cond & (p2 + 1 < n2), *place(p1, p2 + 1))
        send(k, slot, n1 - 2 + p2, cond & (p2 - 1 >= 0), *place(p1, p2 - 1))

    def central(row):
        return (row >= middle[0]) & (row <= middle[1])

    def turn(k):
        slot = i * inner + 1 - j
        wait_blocks(k, 0, 1, central(i), m_recv.at[outer])
        send(k, slot, 0, central(i) & (i + 1 < outer), i + 1, j, m_recv.at[i])
        send(k, slot, 0, central(i) & (i > 0), i - 1, j, m_recv.at[i])

    def pass_on(k, u, closing):
        for step in (-1, 1):
            origin = i + step * u
            valid = (origin >= 0) & (origin < outer) & central(origin)
            origin = jnp.clip(origin, 0, outer - 1)
            onward = i - step
            passed = (onward >= 0) & (onward < outer)
            if closing:
                wait_blocks(k, 0, 1, valid & ~passed, m_recv.at[origin])
            else:
                wait_blocks(k, 0, 1, valid & passed, m_recv.at[origin])
                send(k, origin * inner + 1 - j, 0, valid & passed, onward, j, m_recv.at[origin])

    def own(k):
        n1, n2, p1, p2, slot_of, place = route(k)
        if k % GROUP == 0:
            block = xg.at[pl.ds(0, min(GROUP, units - k))]
            pltpu.make_async_copy(block, block, load_x.at[k // GROUP]).wait()
        send(k, tp, p1, p1 + 1 < n1, *place(p1 + 1, p2))
        send(k, tp, p1 - 1, p1 - 1 >= 0, *place(p1 - 1, p2))
        if k == mixed:
            send(k, tp, 0, central(i), i, 1 - j, m_recv.at[outer])
            cross(k, tp, ~central(i))
        else:
            cross(k, tp, p1 >= 0)

    def line(k, t):
        n1, n2, p1, p2, slot_of, place = route(k)
        for step in (-1, 1):
            origin = p1 + step * t
            valid = (origin >= 0) & (origin < n1)
            origin = jnp.clip(origin, 0, n1 - 1)
            slot = slot_of(origin, p2)
            mark = jnp.clip(origin - (step > 0), 0, n1 - 2)
            wait_blocks(k, mark, 1, valid)
            onward = p1 - step
            send(k, slot, mark, valid & (onward >= 0) & (onward < n1), *place(onward, p2))
            cross(k, slot, valid & ~central(origin) if k == mixed else valid)

    def second_line(k, u, closing):
        n1, n2, p1, p2, slot_of, place = route(k)
        for step in (-1, 1):
            origin = p2 + step * u
            valid = (origin >= 0) & (origin < n2)
            origin = jnp.clip(origin, 0, n2 - 1)
            mark = n1 - 1 + jnp.clip(origin - (step > 0), 0, n2 - 2)
            onward = p2 - step
            passed = (onward >= 0) & (onward < n2) if n2 > 2 else False
            if closing:
                count = n1 - len(middle) if k == mixed else n1
                wait_blocks(k, mark, count, valid & ~passed if n2 > 2 else valid)
            elif n2 > 2:
                wait_blocks(k, mark, n1, valid & passed)
                for r in range(n1):
                    slot = slot_of((p1 + r) % n1, origin)
                    send(k, slot, mark, valid & passed, *place(p1, onward))

    def drain(at_i, at_j):
        totals = [0] * -(-units // BATCH)
        for k in range(units):
            n1, n2, p1, p2 = (inner, outer, at_j, at_i) if k in swapped else (outer, inner, at_i, at_j)
            count = n1 * ((p2 + 1 < n2) + (p2 > 0))
            if k == mixed:
                count -= sum(m != p1 for m in middle)
                count += sum((p1 + 1 < n1) * (m <= p1) + (p1 > 0) * (m >= p1) for m in middle)
            count += (1 + p1) * (p1 + 1 < n1) + (n1 - p1) * (p1 > 0)
            count += n1 * (p2 * (p2 + 1 < n2) + (n2 - 1 - p2) * (p2 > 0))
            totals[k // BATCH] += count
        for n, count in enumerate(totals):
            block = xg.at[pl.ds(0, count)]
            pltpu.make_async_remote_copy(
                block, block, x_send.at[n], x_recv.at[0, 0], device_id=(rep, tp), device_id_type=MESH
            ).wait_send()

    def consume(k):
        c, part = k // SPLIT, k % SPLIT
        s, h = segment_order[c // per_segment], c % per_segment
        at = pl.ds(h * width, width)
        target = gsend.at[s - 1, at] if s else gr.at[0, at]
        product = lax.dot_general(
            xg[pl.ds(k * peers, peers)].reshape(peers * tokens, width), cot[part],
            (((0,), (0,)), ((), ())), preferred_element_type=jnp.float32,
        )
        target[...] = target[...] + product if part else product
        if s and part == SPLIT - 1:
            copy = pltpu.make_async_remote_copy(
                gsend.at[s - 1, at], gr.at[s, at], g_send, g_recv.at[h],
                device_id=(rep ^ s, tp), device_id_type=MESH,
            )
            copy.start()

    pairs = [(s, t) for s in range(replicas) for t in range(s, replicas)]
    fold = gr.shape[2] // LANES

    def inner_products(h, sums):
        piece = gr.at[pl.ds(0, replicas - 1), pl.ds(h * width, width)]
        pltpu.make_async_copy(piece, piece, g_recv.at[h]).wait()

        def products(n, sums):
            at = pl.ds(pl.multiple_of(h * width + n * SUBLANES, SUBLANES), SUBLANES)
            block = [gr[s, at, :] for s in range(replicas)]
            out = []
            for total, (s, t) in zip(sums, pairs):
                prod = block[s] * block[t]
                part = prod[:, :LANES]
                for f in range(1, fold):
                    part = part + prod[:, f * LANES : (f + 1) * LANES]
                out.append(total + part)
            return tuple(out)

        return lax.fori_loop(0, width // SUBLANES, products, sums)

    sums = tuple(jnp.zeros((SUBLANES, LANES), jnp.float32) for _ in pairs)
    loaded = False
    for kind, k, t in timeline(units, outer, inner):
        if kind == "own":
            own(k)
        elif kind == "line":
            line(k, t)
        elif kind == "cross":
            second_line(k, t, False)
        elif kind == "turn":
            turn(k)
        elif kind == "pass":
            pass_on(k, t, False)
        else:
            if not loaded:
                pltpu.make_async_copy(cot, cot, load_g).wait()
                loaded = True
            for u in range(1, route(k)[1]):
                second_line(k, u, True)
            if k == mixed:
                for u in range(1, outer):
                    pass_on(k, u, True)
            consume(k)
            if k == units - 2:
                for h in range(per_segment - 1):
                    sums = inner_products(h, sums)
    sums = inner_products(per_segment - 1, sums)
    lane = lax.broadcasted_iota(jnp.int32, (1, LANES), 1)
    packed = jnp.zeros((1, LANES), jnp.float32)
    for n, total in enumerate(sums):
        packed = jnp.where(lane == n, jnp.sum(total, keepdims=True), packed)
    tile_tp[0] = packed
    for d in range(peers - 1, -1, -1):
        for s in range(replicas - 1, -1, -1):
            if d or s:
                pltpu.make_async_remote_copy(
                    tile_tp.at[0], tile_tp.at[s * peers + d], t_send, t_recv,
                    device_id=(rep ^ s, tp ^ d), device_id_type=MESH,
                ).start()
    pltpu.make_async_copy(states, states, load_s).wait()
    others = tile_tp.at[pl.ds(1, replicas * peers - 1)]
    pltpu.make_async_copy(others, others, t_recv).wait()
    index = {pair: n for n, pair in enumerate(pairs)}
    seen = []
    for s in range(replicas):
        seen.append(jnp.sum(tile_tp[pl.ds(s * peers, peers)], axis=0))
    gram = {}
    for s, t in pairs:
        value = None
        for d in range(replicas):
            p, q = s ^ d, t ^ d
            picked = jnp.where(lane == index[min(p, q), max(p, q)], seen[d], 0.0)
            value = picked if value is None else value + picked
        gram[s, t] = jnp.sum(value, keepdims=True)
    coef = adasum_weights(gram, replicas)
    coef = [jnp.broadcast_to(coef[s], (SUBLANES, gr.shape[2])) for s in range(replicas)]

    masks = []
    mask = replicas // 2
    while mask:
        masks.append(mask)
        mask //= 2
    piece = rows // PIECES

    def w_at(s, q):
        return w_out.at[pl.ds(pl.multiple_of((rep ^ s) * rows + q * piece, piece), piece)]

    last = len(masks) - 1

    def w_send_start(step, s, q):
        m = masks[step]
        pltpu.make_async_remote_copy(
            w_at(s, q), w_at(s, q), w_send, w_last if step == last else w_recv.at[(s ^ m) // 2, q],
            device_id=(rep ^ m, tp), device_id_type=MESH,
        ).start()

    for q in range(PIECES):
        def update(n, carry):
            at = pl.ds(pl.multiple_of(q * piece + n * SUBLANES * 2, SUBLANES * 2), SUBLANES * 2)
            value = None
            for s in range(replicas):
                term = coef[s][:1] * gr[s, at, :]
                value = term if value is None else value + term
            moment_new = BETA_ONE * states[1, at, :] + (1.0 - BETA_ONE) * value
            second_new = BETA_TWO * states[2, at, :] + (1.0 - BETA_TWO) * value * value
            master_new = states[0, at, :] - LEARN * (moment_new / CORRECT_ONE) / (
                jnp.sqrt(second_new / CORRECT_TWO) + 1e-08
            )
            comb[at, :] = value
            mom[at, :] = moment_new
            sec[at, :] = second_new
            mas[at, :] = master_new
            own_at = pl.ds(pl.multiple_of(rep * rows + q * piece + n * SUBLANES * 2, SUBLANES * 2), SUBLANES * 2)
            w_out[own_at, :] = master_new.astype(jnp.bfloat16)
            return carry

        lax.fori_loop(0, piece // (SUBLANES * 2), update, 0)
        for step in range(len(masks)):
            w_send_start(step, 0, q)
    def relay(q, step, s):
        pltpu.make_async_copy(w_at(s, q), w_at(s, q), w_recv.at[s // 2, q]).wait()
        for later in range(step + 1, len(masks)):
            w_send_start(later, s, q)

    held = [0]
    for step, m in enumerate(masks[:-1]):
        fresh = [s ^ m for s in held]
        for q in range(PIECES):
            for s in fresh:
                relay(q, step, s)
        held = held + fresh

    half = w_out.at[pl.ds(0, replicas // 2 * rows)]
    pltpu.make_async_copy(half, half, w_last).wait()
    for at_i in range(outer):
        for at_j in range(inner):
            pl.when((i == at_i) & (j == at_j))(functools.partial(drain, at_i, at_j))
    pltpu.make_async_copy(gsend, gsend, g_send).wait()
    pltpu.make_async_copy(others, others, t_send).wait()
    sent = w_out.at[pl.ds(0, (replicas - 1) * rows)]
    pltpu.make_async_copy(sent, sent, w_send).wait()


def deliver(*refs):
    sources, targets, sem = refs[:5], refs[5:10], refs[10]
    for n, (src, dst) in enumerate(zip(sources, targets)):
        step = src.shape[0] // PIECES
        for q in range(PIECES):
            at = pl.ds(q * step, step)
            pltpu.make_async_copy(src.at[at], dst.at[at], sem.at[n]).start()
    for n, (src, dst) in enumerate(zip(sources, targets)):
        pltpu.make_async_copy(src, dst, sem.at[n]).wait()


def per_device(inputs, cotangent, master, moment, second):
    replicas = lax.axis_size("rep")
    peers = lax.axis_size("tp")
    inner = 1 << (peers.bit_length() - 1) // 2
    outer = peers // inner
    tokens, depth = inputs.shape
    features = cotangent.shape[1]
    rows = depth // replicas
    width = min(LANES, rows)
    chunks = depth // width
    per_segment = rows // width
    units = chunks * SPLIT
    anywhere = pl.BlockSpec(memory_space=pl.ANY)
    vmem = pl.BlockSpec(memory_space=pltpu.VMEM)
    dma = pltpu.SemaphoreType.DMA
    small = pltpu.VMEM((rows, features), jnp.float32)
    results = pl.pallas_call(
        functools.partial(kernel, replicas, outer, inner),
        out_shape=(small, small, small, small, pltpu.VMEM((depth, features), jnp.bfloat16)),
        in_specs=[anywhere] * 5,
        out_specs=(vmem,) * 5,
        scratch_shapes=[
            pltpu.VMEM((units * peers, tokens // SPLIT, width), jnp.bfloat16),
            pltpu.VMEM((SPLIT, cotangent.shape[0] // SPLIT, features), jnp.bfloat16),
            pltpu.VMEM((replicas - 1, rows, features), jnp.float32),
            pltpu.VMEM((replicas, rows, features), jnp.float32),
            pltpu.VMEM((3, rows, features), jnp.float32),
            pltpu.VMEM((replicas * peers, 1, LANES), jnp.float32),
            dma((-(-units // GROUP),)),
            dma(()),
            dma(()),
            dma((-(-units // BATCH),)),
            dma((units, outer + inner - 2)),
            dma((outer + 1,)),
            dma(()),
            dma((per_segment,)),
            dma(()),
            dma(()),
            dma(()),
            dma((replicas // 2, PIECES)),
            dma(()),
        ],
        compiler_params=pltpu.CompilerParams(
            collective_id=0, has_side_effects=True, vmem_limit_bytes=48 * 1024 * 1024
        ),
        name="adasum_adam",
    )(inputs, cotangent, master, moment, second)
    results = [pltpu.with_memory_space_constraint(r, pltpu.VMEM) for r in results]
    return pl.pallas_call(
        deliver,
        out_shape=tuple(jax.ShapeDtypeStruct(r.shape, r.dtype) for r in results),
        in_specs=[vmem] * 5,
        out_specs=(anywhere,) * 5,
        scratch_shapes=[dma((5,))],
        compiler_params=pltpu.CompilerParams(vmem_limit_bytes=1024 * 1024),
        name="deliver",
    )(*results)


def solution(mesh):
    return jax.shard_map(
        per_device,
        mesh=mesh,
        in_specs=(
            P(("rep", "tp"), None),
            P("rep", "tp"),
            P("rep", "tp"),
            P("rep", "tp"),
            P("rep", "tp"),
        ),
        out_specs=(P("rep", "tp"), P("rep", "tp"), P("rep", "tp"), P("rep", "tp"), P(None, "tp")),
        check_vma=False,
    )
```

```python
import functools
import jax
import jax.numpy as jnp
from jax import lax
from jax.experimental import pallas as pl
from jax.experimental.pallas import tpu as pltpu
from jax.sharding import PartitionSpec as P

EPS_SUM = 1e-06
BETA_ONE = 0.9
BETA_TWO = 0.999
LEARN = 0.01
CORRECT_ONE = 1.0 - 0.9**50
CORRECT_TWO = 1.0 - 0.999**50
LANES = 128
SUBLANES = 8
PIECES = 8
SPLIT = 2
OWN_LEAD = 7
LINE_LEAD = (4.5, 3.5, 2.5)
SWAP_LEAD = (4.5,)
LINE_CROSS = (0,)
SWAP_CROSS = (2.0, 1.5, 1.5)
SWAPPED = (9, 14)
GROUP = 4
BATCH = 8
MIXED = (4, 11)
MESH = pl.DeviceIdType.MESH


def adasum_weights(gram, replicas):
    entries = [{s: jnp.ones((1, 1), jnp.float32)} for s in range(replicas)]

    def inner(left, right):
        total = None
        for i, u in left.items():
            for j, v in right.items():
                term = (u * v) * gram[min(i, j), max(i, j)]
                total = term if total is None else total + term
        return total

    while len(entries) > 1:
        half = len(entries) // 2
        merged = []
        for a, b in zip(entries[:half], entries[half:]):
            aa, bb, ab = inner(a, a), inner(b, b), inner(a, b)
            ca = 1.0 - ab / (2.0 * (aa + EPS_SUM))
            cb = 1.0 - ab / (2.0 * (bb + EPS_SUM))
            merged.append({**{i: ca * u for i, u in a.items()}, **{i: cb * u for i, u in b.items()}})
        entries = merged
    return entries[0]


def timeline(units, outer, inner):
    steps = []
    for k in range(units):
        mixed = k in MIXED and inner == 2
        swap = not mixed and k in SWAPPED + MIXED
        n1, n2 = (inner, outer) if swap else (outer, inner)
        steps.append((k - OWN_LEAD, 0, "own", k, 0))
        lead = SWAP_LEAD if swap else LINE_LEAD
        late = k - OWN_LEAD
        for t in range(1, n1):
            late = max(late, k - lead[min(t, len(lead)) - 1])
            steps.append((late, t, "line", k, t))
        if mixed:
            turn = max(k - OWN_LEAD, k - SWAP_LEAD[0])
            steps.append((turn, 0.5, "turn", k, 0))
            for u in range(1, n1):
                turn = max(turn, k - SWAP_CROSS[min(u, len(SWAP_CROSS)) - 1])
                steps.append((turn, n1 + u, "pass", k, u))
        lead = SWAP_CROSS if swap else LINE_CROSS
        for u in range(1, n2):
            late = max(late, k - lead[min(u, len(lead)) - 1])
            steps.append((late, n1 + u, "cross", k, u))
        steps.append((max(late, k), n1 + n2, "consume", k, 0))
    return [step[2:] for step in sorted(steps)]


def kernel(
    replicas, outer, inner,
    x_hbm, g_hbm, master_hbm, moment_hbm, second_hbm,
    comb, mom, sec, mas, w_out,
    xg, cot, gsend, gr, states, tile_tp,
    load_x, load_g, load_s, x_send, x_recv, m_recv, g_send, g_recv, t_send, t_recv, w_send, w_recv, w_last,
):
    rep = lax.axis_index("rep")
    tp = lax.axis_index("tp")
    peers = outer * inner
    i, j = tp // inner, tp % inner
    units = xg.shape[0] // peers
    tokens, width = xg.shape[1], xg.shape[2]
    swapped = SWAPPED if inner == 2 else SWAPPED + MIXED
    mixed = MIXED if inner == 2 else ()
    edges = (0, outer - 1)
    chunks = units // SPLIT
    per_segment = chunks // replicas
    segment_order = list(range(replicas - 1, -1, -1))
    rows = gr.shape[1]

    for k in range(units):
        c, part = k // SPLIT, k % SPLIT
        s, h = segment_order[c // per_segment], c % per_segment
        column = pl.multiple_of(((rep ^ s) * per_segment + h) * width, width)
        source = x_hbm.at[pl.ds(part * tokens, tokens), pl.ds(column, width)]
        pltpu.make_async_copy(source, xg.at[k * peers + tp], load_x.at[k // GROUP]).start()

    barrier = pltpu.get_barrier_semaphore()
    greeted = replicas - 1
    for ok, to_i, to_j in ((i > 0, i - 1, j), (i + 1 < outer, i + 1, j), (j > 0, i, j - 1), (j + 1 < inner, i, j + 1)):
        target = jnp.clip(to_i, 0, outer - 1) * inner + jnp.clip(to_j, 0, inner - 1)

        @pl.when(ok)
        def _():
            pl.semaphore_signal(barrier, inc=1, device_id=(rep, target), device_id_type=MESH)

        greeted = greeted + jnp.where(ok, 1, 0)
    for s in range(1, replicas):
        pl.semaphore_signal(barrier, inc=1, device_id=(rep ^ s, tp), device_id_type=MESH)

    for part in range(SPLIT):
        for slot in range(peers):
            source = g_hbm.at[pl.ds((slot * SPLIT + part) * tokens, tokens)]
            pltpu.make_async_copy(source, cot.at[part, pl.ds(slot * tokens, tokens)], load_g).start()
    for n, source in enumerate((master_hbm, moment_hbm, second_hbm)):
        pltpu.make_async_copy(source, states.at[n], load_s).start()
    pl.semaphore_wait(barrier, greeted)

    def send(k, slot, mark, cond, to_i, to_j, arrived=None):
        target = jnp.clip(to_i, 0, outer - 1) * inner + jnp.clip(to_j, 0, inner - 1)
        block = xg.at[k * peers + slot]

        @pl.when(cond)
        def _():
            pltpu.make_async_remote_copy(
                block, block, x_send.at[k // BATCH], x_recv.at[k, mark] if arrived is None else arrived, device_id=(rep, target), device_id_type=MESH
            ).start()

    def wait_blocks(k, mark, count, cond, arrived=None):
        block = xg.at[pl.ds(k * peers, count)]

        @pl.when(cond)
        def _():
            pltpu.make_async_remote_copy(
                block, block, x_send.at[0], x_recv.at[k, mark] if arrived is None else arrived, device_id=(rep, tp), device_id_type=MESH
            ).wait_recv()

    def route(k):
        if k in swapped:
            return inner, outer, j, i, lambda q1, q2: q2 * inner + q1, lambda q1, q2: (q2, q1)
        return outer, inner, i, j, lambda q1, q2: q1 * inner + q2, lambda q1, q2: (q1, q2)

    def cross(k, slot, cond):
        n1, n2, p1, p2, slot_of, place = route(k)
        send(k, slot, n1 - 1 + p2, cond & (p2 + 1 < n2), *place(p1, p2 + 1))
        send(k, slot, n1 - 2 + p2, cond & (p2 - 1 >= 0), *place(p1, p2 - 1))

    def at_edge(row):
        return (row == edges[0]) | (row == edges[1])

    def turn(k):
        slot = i * inner + 1 - j
        wait_blocks(k, 0, 1, at_edge(i), m_recv.at[mixed.index(k), outer])
        send(k, slot, 0, at_edge(i) & (i + 1 < outer), i + 1, j, m_recv.at[mixed.index(k), i])
        send(k, slot, 0, at_edge(i) & (i > 0), i - 1, j, m_recv.at[mixed.index(k), i])

    def pass_on(k, u, closing):
        for step in (-1, 1):
            origin = i + step * u
            valid = (origin >= 0) & (origin < outer) & at_edge(origin)
            origin = jnp.clip(origin, 0, outer - 1)
            onward = i - step
            passed = (onward >= 0) & (onward < outer)
            if closing:
                wait_blocks(k, 0, 1, valid & ~passed, m_recv.at[mixed.index(k), origin])
            else:
                wait_blocks(k, 0, 1, valid & passed, m_recv.at[mixed.index(k), origin])
                send(k, origin * inner + 1 - j, 0, valid & passed, onward, j, m_recv.at[mixed.index(k), origin])

    def own(k):
        n1, n2, p1, p2, slot_of, place = route(k)
        if k % GROUP == 0:
            block = xg.at[pl.ds(0, min(GROUP, units - k))]
            pltpu.make_async_copy(block, block, load_x.at[k // GROUP]).wait()
        send(k, tp, p1, p1 + 1 < n1, *place(p1 + 1, p2))
        send(k, tp, p1 - 1, p1 - 1 >= 0, *place(p1 - 1, p2))
        if k in mixed:
            send(k, tp, 0, at_edge(i), i, 1 - j, m_recv.at[mixed.index(k), outer])
            cross(k, tp, ~at_edge(i))
        else:
            cross(k, tp, p1 >= 0)

    def line(k, t):
        n1, n2, p1, p2, slot_of, place = route(k)
        for step in (-1, 1):
            origin = p1 + step * t
            valid = (origin >= 0) & (origin < n1)
            origin = jnp.clip(origin, 0, n1 - 1)
            slot = slot_of(origin, p2)
            mark = jnp.clip(origin - (step > 0), 0, n1 - 2)
            wait_blocks(k, mark, 1, valid)
            onward = p1 - step
            send(k, slot, mark, valid & (onward >= 0) & (onward < n1), *place(onward, p2))
            cross(k, slot, valid & ~at_edge(origin) if k in mixed else valid)

    def second_line(k, u, closing):
        n1, n2, p1, p2, slot_of, place = route(k)
        for step in (-1, 1):
            origin = p2 + step * u
            valid = (origin >= 0) & (origin < n2)
            origin = jnp.clip(origin, 0, n2 - 1)
            mark = n1 - 1 + jnp.clip(origin - (step > 0), 0, n2 - 2)
            onward = p2 - step
            passed = (onward >= 0) & (onward < n2) if n2 > 2 else False
            if closing:
                count = n1 - len(edges) if k in mixed else n1
                wait_blocks(k, mark, count, valid & ~passed if n2 > 2 else valid)
            elif n2 > 2:
                wait_blocks(k, mark, n1, valid & passed)
                for r in range(n1):
                    slot = slot_of((p1 + r) % n1, origin)
                    send(k, slot, mark, valid & passed, *place(p1, onward))

    def drain(at_i, at_j):
        totals = [0] * -(-units // BATCH)
        for k in range(units):
            n1, n2, p1, p2 = (inner, outer, at_j, at_i) if k in swapped else (outer, inner, at_i, at_j)
            count = n1 * ((p2 + 1 < n2) + (p2 > 0))
            if k in mixed:
                count -= sum(m != p1 for m in edges)
                count += sum((p1 + 1 < n1) * (m <= p1) + (p1 > 0) * (m >= p1) for m in edges)
            count += (1 + p1) * (p1 + 1 < n1) + (n1 - p1) * (p1 > 0)
            count += n1 * (p2 * (p2 + 1 < n2) + (n2 - 1 - p2) * (p2 > 0))
            totals[k // BATCH] += count
        for n, count in enumerate(totals):
            block = xg.at[pl.ds(0, count)]
            pltpu.make_async_remote_copy(
                block, block, x_send.at[n], x_recv.at[0, 0], device_id=(rep, tp), device_id_type=MESH
            ).wait_send()

    def consume(k):
        c, part = k // SPLIT, k % SPLIT
        s, h = segment_order[c // per_segment], c % per_segment
        at = pl.ds(h * width, width)
        target = gsend.at[s - 1, at] if s else gr.at[0, at]
        product = lax.dot_general(
            xg[pl.ds(k * peers, peers)].reshape(peers * tokens, width), cot[part],
            (((0,), (0,)), ((), ())), preferred_element_type=jnp.float32,
        )
        target[...] = target[...] + product if part else product
        if s and part == SPLIT - 1:
            copy = pltpu.make_async_remote_copy(
                gsend.at[s - 1, at], gr.at[s, at], g_send, g_recv.at[h],
                device_id=(rep ^ s, tp), device_id_type=MESH,
            )
            copy.start()

    pairs = [(s, t) for s in range(replicas) for t in range(s, replicas)]
    fold = gr.shape[2] // LANES

    def inner_products(h, sums, chosen, fresh=True):
        if fresh:
            piece = gr.at[pl.ds(0, replicas - 1), pl.ds(h * width, width)]
            pltpu.make_async_copy(piece, piece, g_recv.at[h]).wait()

        def products(n, sums):
            at = pl.ds(pl.multiple_of(h * width + n * SUBLANES, SUBLANES), SUBLANES)
            block = {s: gr[s, at, :] for s in sorted({m for pair in chosen for m in pair})}
            out = []
            for total, (s, t) in zip(sums, pairs):
                if (s, t) not in chosen:
                    out.append(total)
                    continue
                prod = block[s] * block[t]
                part = prod[:, :LANES]
                for f in range(1, fold):
                    part = part + prod[:, f * LANES : (f + 1) * LANES]
                out.append(total + part)
            return tuple(out)

        return lax.fori_loop(0, width // SUBLANES, products, sums)

    sums = tuple(jnp.zeros((SUBLANES, LANES), jnp.float32) for _ in pairs)
    loaded = False
    for kind, k, t in timeline(units, outer, inner):
        if kind == "own":
            own(k)
        elif kind == "line":
            line(k, t)
        elif kind == "cross":
            second_line(k, t, False)
        elif kind == "turn":
            turn(k)
        elif kind == "pass":
            pass_on(k, t, False)
        else:
            if not loaded:
                pltpu.make_async_copy(cot, cot, load_g).wait()
                loaded = True
            for u in range(1, route(k)[1]):
                second_line(k, u, True)
            if k in mixed:
                for u in range(1, outer):
                    pass_on(k, u, True)
            consume(k)
            if k == units - SPLIT - 1:
                for h in range(per_segment - 1):
                    sums = inner_products(h, sums, pairs)
                sums = inner_products(per_segment - 1, sums, [pair for pair in pairs if pair[0]])
    sums = inner_products(per_segment - 1, sums, [pair for pair in pairs if not pair[0]], False)
    lane = lax.broadcasted_iota(jnp.int32, (1, LANES), 1)
    packed = jnp.zeros((1, LANES), jnp.float32)
    for n, total in enumerate(sums):
        packed = jnp.where(lane == n, jnp.sum(total, keepdims=True), packed)
    tile_tp[0] = packed
    for d in range(peers - 1, -1, -1):
        for s in range(replicas - 1, -1, -1):
            if d or s:
                pltpu.make_async_remote_copy(
                    tile_tp.at[0], tile_tp.at[s * peers + d], t_send, t_recv,
                    device_id=(rep ^ s, tp ^ d), device_id_type=MESH,
                ).start()
    pltpu.make_async_copy(states, states, load_s).wait()
    others = tile_tp.at[pl.ds(1, replicas * peers - 1)]
    pltpu.make_async_copy(others, others, t_recv).wait()
    index = {pair: n for n, pair in enumerate(pairs)}
    seen = []
    for s in range(replicas):
        seen.append(jnp.sum(tile_tp[pl.ds(s * peers, peers)], axis=0))
    gram = {}
    for s, t in pairs:
        value = None
        for d in range(replicas):
            p, q = s ^ d, t ^ d
            picked = jnp.where(lane == index[min(p, q), max(p, q)], seen[d], 0.0)
            value = picked if value is None else value + picked
        gram[s, t] = jnp.sum(value, keepdims=True)
    coef = adasum_weights(gram, replicas)
    coef = [jnp.broadcast_to(coef[s], (SUBLANES, gr.shape[2])) for s in range(replicas)]

    masks = []
    mask = replicas // 2
    while mask:
        masks.append(mask)
        mask //= 2
    piece = rows // PIECES

    def w_at(s, q):
        return w_out.at[pl.ds(pl.multiple_of((rep ^ s) * rows + q * piece, piece), piece)]

    last = len(masks) - 1

    def w_send_start(step, s, q):
        m = masks[step]
        pltpu.make_async_remote_copy(
            w_at(s, q), w_at(s, q), w_send, w_last if step == last else w_recv.at[(s ^ m) // 2, q],
            device_id=(rep ^ m, tp), device_id_type=MESH,
        ).start()

    for q in range(PIECES):
        def update(n, carry):
            at = pl.ds(pl.multiple_of(q * piece + n * SUBLANES * 2, SUBLANES * 2), SUBLANES * 2)
            value = None
            for s in range(replicas):
                term = coef[s][:1] * gr[s, at, :]
                value = term if value is None else value + term
            moment_new = BETA_ONE * states[1, at, :] + (1.0 - BETA_ONE) * value
            second_new = BETA_TWO * states[2, at, :] + (1.0 - BETA_TWO) * value * value
            master_new = states[0, at, :] - LEARN * (moment_new / CORRECT_ONE) / (
                jnp.sqrt(second_new / CORRECT_TWO) + 1e-08
            )
            comb[at, :] = value
            mom[at, :] = moment_new
            sec[at, :] = second_new
            mas[at, :] = master_new
            own_at = pl.ds(pl.multiple_of(rep * rows + q * piece + n * SUBLANES * 2, SUBLANES * 2), SUBLANES * 2)
            w_out[own_at, :] = master_new.astype(jnp.bfloat16)
            return carry

        lax.fori_loop(0, piece // (SUBLANES * 2), update, 0)
        for step in range(len(masks)):
            w_send_start(step, 0, q)
    def relay(q, step, s):
        pltpu.make_async_copy(w_at(s, q), w_at(s, q), w_recv.at[s // 2, q]).wait()
        for later in range(step + 1, len(masks)):
            w_send_start(later, s, q)

    held = [0]
    for step, m in enumerate(masks[:-1]):
        fresh = [s ^ m for s in held]
        for q in range(PIECES):
            for s in fresh:
                relay(q, step, s)
        held = held + fresh

    half = w_out.at[pl.ds(0, replicas // 2 * rows)]
    pltpu.make_async_copy(half, half, w_last).wait()
    for at_i in range(outer):
        for at_j in range(inner):
            pl.when((i == at_i) & (j == at_j))(functools.partial(drain, at_i, at_j))
    pltpu.make_async_copy(gsend, gsend, g_send).wait()
    pltpu.make_async_copy(others, others, t_send).wait()
    sent = w_out.at[pl.ds(0, (replicas - 1) * rows)]
    pltpu.make_async_copy(sent, sent, w_send).wait()


def deliver(*refs):
    sources, targets, sem = refs[:5], refs[5:10], refs[10]
    for n, (src, dst) in enumerate(zip(sources, targets)):
        step = src.shape[0] // PIECES
        for q in range(PIECES):
            at = pl.ds(q * step, step)
            pltpu.make_async_copy(src.at[at], dst.at[at], sem.at[n]).start()
    for n, (src, dst) in enumerate(zip(sources, targets)):
        pltpu.make_async_copy(src, dst, sem.at[n]).wait()


def per_device(inputs, cotangent, master, moment, second):
    replicas = lax.axis_size("rep")
    peers = lax.axis_size("tp")
    inner = 1 << (peers.bit_length() - 1) // 2
    outer = peers // inner
    tokens, depth = inputs.shape
    features = cotangent.shape[1]
    rows = depth // replicas
    width = min(LANES, rows)
    chunks = depth // width
    per_segment = rows // width
    units = chunks * SPLIT
    anywhere = pl.BlockSpec(memory_space=pl.ANY)
    vmem = pl.BlockSpec(memory_space=pltpu.VMEM)
    dma = pltpu.SemaphoreType.DMA
    small = pltpu.VMEM((rows, features), jnp.float32)
    results = pl.pallas_call(
        functools.partial(kernel, replicas, outer, inner),
        out_shape=(small, small, small, small, pltpu.VMEM((depth, features), jnp.bfloat16)),
        in_specs=[anywhere] * 5,
        out_specs=(vmem,) * 5,
        scratch_shapes=[
            pltpu.VMEM((units * peers, tokens // SPLIT, width), jnp.bfloat16),
            pltpu.VMEM((SPLIT, cotangent.shape[0] // SPLIT, features), jnp.bfloat16),
            pltpu.VMEM((replicas - 1, rows, features), jnp.float32),
            pltpu.VMEM((replicas, rows, features), jnp.float32),
            pltpu.VMEM((3, rows, features), jnp.float32),
            pltpu.VMEM((replicas * peers, 1, LANES), jnp.float32),
            dma((-(-units // GROUP),)),
            dma(()),
            dma(()),
            dma((-(-units // BATCH),)),
            dma((units, outer + inner - 2)),
            dma((len(MIXED), outer + 1)),
            dma(()),
            dma((per_segment,)),
            dma(()),
            dma(()),
            dma(()),
            dma((replicas // 2, PIECES)),
            dma(()),
        ],
        compiler_params=pltpu.CompilerParams(
            collective_id=0, has_side_effects=True, vmem_limit_bytes=48 * 1024 * 1024
        ),
        name="adasum_adam",
    )(inputs, cotangent, master, moment, second)
    results = [pltpu.with_memory_space_constraint(r, pltpu.VMEM) for r in results]
    return pl.pallas_call(
        deliver,
        out_shape=tuple(jax.ShapeDtypeStruct(r.shape, r.dtype) for r in results),
        in_specs=[vmem] * 5,
        out_specs=(anywhere,) * 5,
        scratch_shapes=[dma((5,))],
        compiler_params=pltpu.CompilerParams(vmem_limit_bytes=1024 * 1024),
        name="deliver",
    )(*results)


def solution(mesh):
    return jax.shard_map(
        per_device,
        mesh=mesh,
        in_specs=(
            P(("rep", "tp"), None),
            P("rep", "tp"),
            P("rep", "tp"),
            P("rep", "tp"),
            P("rep", "tp"),
        ),
        out_specs=(P("rep", "tp"), P("rep", "tp"), P("rep", "tp"), P("rep", "tp"), P(None, "tp")),
        check_vma=False,
    )
```

```python
import functools
import jax
import jax.numpy as jnp
from jax import lax
from jax.experimental import pallas as pl
from jax.experimental.pallas import tpu as pltpu
from jax.sharding import PartitionSpec as P

EPS_SUM = 1e-06
BETA_ONE = 0.9
BETA_TWO = 0.999
LEARN = 0.01
CORRECT_ONE = 1.0 - 0.9**50
CORRECT_TWO = 1.0 - 0.999**50
LANES = 128
SUBLANES = 8
PIECES = 16
SPLIT = 2
OWN_LEAD = 7
LINE_LEAD = (4.5, 3.5, 2.5)
SWAP_LEAD = (4.5,)
LINE_CROSS = (0,)
SWAP_CROSS = (2.0, 1.5, 1.5)
SWAPPED = (9, 14)
GROUP = 4
BATCH = 8
MIXED = (4, 11)
MESH = pl.DeviceIdType.MESH


def adasum_weights(gram, replicas):
    entries = [{s: jnp.ones((1, 1), jnp.float32)} for s in range(replicas)]

    def inner(left, right):
        total = None
        for i, u in left.items():
            for j, v in right.items():
                term = (u * v) * gram[min(i, j), max(i, j)]
                total = term if total is None else total + term
        return total

    while len(entries) > 1:
        half = len(entries) // 2
        merged = []
        for a, b in zip(entries[:half], entries[half:]):
            aa, bb, ab = inner(a, a), inner(b, b), inner(a, b)
            ca = 1.0 - ab / (2.0 * (aa + EPS_SUM))
            cb = 1.0 - ab / (2.0 * (bb + EPS_SUM))
            merged.append({**{i: ca * u for i, u in a.items()}, **{i: cb * u for i, u in b.items()}})
        entries = merged
    return entries[0]


def timeline(units, outer, inner):
    steps = []
    for k in range(units):
        mixed = k in MIXED and inner == 2
        swap = not mixed and k in SWAPPED + MIXED
        n1, n2 = (inner, outer) if swap else (outer, inner)
        steps.append((k - OWN_LEAD, 0, "own", k, 0))
        lead = SWAP_LEAD if swap else LINE_LEAD
        late = k - OWN_LEAD
        for t in range(1, n1):
            late = max(late, k - lead[min(t, len(lead)) - 1])
            steps.append((late, t, "line", k, t))
        if mixed:
            turn = max(k - OWN_LEAD, k - SWAP_LEAD[0])
            steps.append((turn, 0.5, "turn", k, 0))
            for u in range(1, n1):
                turn = max(turn, k - SWAP_CROSS[min(u, len(SWAP_CROSS)) - 1])
                steps.append((turn, n1 + u, "pass", k, u))
        lead = SWAP_CROSS if swap else LINE_CROSS
        for u in range(1, n2):
            late = max(late, k - lead[min(u, len(lead)) - 1])
            steps.append((late, n1 + u, "cross", k, u))
        steps.append((max(late, k), n1 + n2, "consume", k, 0))
    return [step[2:] for step in sorted(steps)]


def kernel(
    replicas, outer, inner,
    x_hbm, g_hbm, master_hbm, moment_hbm, second_hbm,
    comb, mom, sec, mas, w_out,
    xg, cot, gsend, gr, states, tile_tp,
    load_x, load_g, load_s, x_send, x_recv, m_recv, g_send, g_recv, t_send, t_recv, w_send, w_recv, w_last,
):
    rep = lax.axis_index("rep")
    tp = lax.axis_index("tp")
    peers = outer * inner
    i, j = tp // inner, tp % inner
    units = xg.shape[0] // peers
    tokens, width = xg.shape[1], xg.shape[2]
    swapped = SWAPPED if inner == 2 else SWAPPED + MIXED
    mixed = MIXED if inner == 2 else ()
    edges = (0, outer - 1)
    chunks = units // SPLIT
    per_segment = chunks // replicas
    segment_order = list(range(replicas - 1, -1, -1))
    rows = gr.shape[1]

    for k in range(units):
        c, part = k // SPLIT, k % SPLIT
        s, h = segment_order[c // per_segment], c % per_segment
        column = pl.multiple_of(((rep ^ s) * per_segment + h) * width, width)
        source = x_hbm.at[pl.ds(part * tokens, tokens), pl.ds(column, width)]
        pltpu.make_async_copy(source, xg.at[k * peers + tp], load_x.at[k // GROUP]).start()

    barrier = pltpu.get_barrier_semaphore()
    greeted = replicas - 1
    for ok, to_i, to_j in ((i > 0, i - 1, j), (i + 1 < outer, i + 1, j), (j > 0, i, j - 1), (j + 1 < inner, i, j + 1)):
        target = jnp.clip(to_i, 0, outer - 1) * inner + jnp.clip(to_j, 0, inner - 1)

        @pl.when(ok)
        def _():
            pl.semaphore_signal(barrier, inc=1, device_id=(rep, target), device_id_type=MESH)

        greeted = greeted + jnp.where(ok, 1, 0)
    for s in range(1, replicas):
        pl.semaphore_signal(barrier, inc=1, device_id=(rep ^ s, tp), device_id_type=MESH)

    for part in range(SPLIT):
        for slot in range(peers):
            source = g_hbm.at[pl.ds((slot * SPLIT + part) * tokens, tokens)]
            pltpu.make_async_copy(source, cot.at[part, pl.ds(slot * tokens, tokens)], load_g).start()
    for n, source in enumerate((master_hbm, moment_hbm, second_hbm)):
        pltpu.make_async_copy(source, states.at[n], load_s).start()
    pl.semaphore_wait(barrier, greeted)

    def send(k, slot, mark, cond, to_i, to_j, arrived=None):
        target = jnp.clip(to_i, 0, outer - 1) * inner + jnp.clip(to_j, 0, inner - 1)
        block = xg.at[k * peers + slot]

        @pl.when(cond)
        def _():
            pltpu.make_async_remote_copy(
                block, block, x_send.at[k // BATCH], x_recv.at[k, mark] if arrived is None else arrived, device_id=(rep, target), device_id_type=MESH
            ).start()

    def wait_blocks(k, mark, count, cond, arrived=None):
        block = xg.at[pl.ds(k * peers, count)]

        @pl.when(cond)
        def _():
            pltpu.make_async_remote_copy(
                block, block, x_send.at[0], x_recv.at[k, mark] if arrived is None else arrived, device_id=(rep, tp), device_id_type=MESH
            ).wait_recv()

    def route(k):
        if k in swapped:
            return inner, outer, j, i, lambda q1, q2: q2 * inner + q1, lambda q1, q2: (q2, q1)
        return outer, inner, i, j, lambda q1, q2: q1 * inner + q2, lambda q1, q2: (q1, q2)

    def cross(k, slot, cond):
        n1, n2, p1, p2, slot_of, place = route(k)
        send(k, slot, n1 - 1 + p2, cond & (p2 + 1 < n2), *place(p1, p2 + 1))
        send(k, slot, n1 - 2 + p2, cond & (p2 - 1 >= 0), *place(p1, p2 - 1))

    def at_edge(row):
        return (row == edges[0]) | (row == edges[1])

    def turn(k):
        slot = i * inner + 1 - j
        wait_blocks(k, 0, 1, at_edge(i), m_recv.at[mixed.index(k), outer])
        send(k, slot, 0, at_edge(i) & (i + 1 < outer), i + 1, j, m_recv.at[mixed.index(k), i])
        send(k, slot, 0, at_edge(i) & (i > 0), i - 1, j, m_recv.at[mixed.index(k), i])

    def pass_on(k, u, closing):
        for step in (-1, 1):
            origin = i + step * u
            valid = (origin >= 0) & (origin < outer) & at_edge(origin)
            origin = jnp.clip(origin, 0, outer - 1)
            onward = i - step
            passed = (onward >= 0) & (onward < outer)
            if closing:
                wait_blocks(k, 0, 1, valid & ~passed, m_recv.at[mixed.index(k), origin])
            else:
                wait_blocks(k, 0, 1, valid & passed, m_recv.at[mixed.index(k), origin])
                send(k, origin * inner + 1 - j, 0, valid & passed, onward, j, m_recv.at[mixed.index(k), origin])

    def own(k):
        n1, n2, p1, p2, slot_of, place = route(k)
        if k % GROUP == 0:
            block = xg.at[pl.ds(0, min(GROUP, units - k))]
            pltpu.make_async_copy(block, block, load_x.at[k // GROUP]).wait()
        send(k, tp, p1, p1 + 1 < n1, *place(p1 + 1, p2))
        send(k, tp, p1 - 1, p1 - 1 >= 0, *place(p1 - 1, p2))
        if k in mixed:
            send(k, tp, 0, at_edge(i), i, 1 - j, m_recv.at[mixed.index(k), outer])
            cross(k, tp, ~at_edge(i))
        else:
            cross(k, tp, p1 >= 0)

    def line(k, t):
        n1, n2, p1, p2, slot_of, place = route(k)
        for step in (-1, 1):
            origin = p1 + step * t
            valid = (origin >= 0) & (origin < n1)
            origin = jnp.clip(origin, 0, n1 - 1)
            slot = slot_of(origin, p2)
            mark = jnp.clip(origin - (step > 0), 0, n1 - 2)
            wait_blocks(k, mark, 1, valid)
            onward = p1 - step
            send(k, slot, mark, valid & (onward >= 0) & (onward < n1), *place(onward, p2))
            cross(k, slot, valid & ~at_edge(origin) if k in mixed else valid)

    def second_line(k, u, closing):
        n1, n2, p1, p2, slot_of, place = route(k)
        for step in (-1, 1):
            origin = p2 + step * u
            valid = (origin >= 0) & (origin < n2)
            origin = jnp.clip(origin, 0, n2 - 1)
            mark = n1 - 1 + jnp.clip(origin - (step > 0), 0, n2 - 2)
            onward = p2 - step
            passed = (onward >= 0) & (onward < n2) if n2 > 2 else False
            if closing:
                count = n1 - len(edges) if k in mixed else n1
                wait_blocks(k, mark, count, valid & ~passed if n2 > 2 else valid)
            elif n2 > 2:
                wait_blocks(k, mark, n1, valid & passed)
                for r in range(n1):
                    slot = slot_of((p1 + r) % n1, origin)
                    send(k, slot, mark, valid & passed, *place(p1, onward))

    def drain(at_i, at_j):
        totals = [0] * -(-units // BATCH)
        for k in range(units):
            n1, n2, p1, p2 = (inner, outer, at_j, at_i) if k in swapped else (outer, inner, at_i, at_j)
            count = n1 * ((p2 + 1 < n2) + (p2 > 0))
            if k in mixed:
                count -= sum(m != p1 for m in edges)
                count += sum((p1 + 1 < n1) * (m <= p1) + (p1 > 0) * (m >= p1) for m in edges)
            count += (1 + p1) * (p1 + 1 < n1) + (n1 - p1) * (p1 > 0)
            count += n1 * (p2 * (p2 + 1 < n2) + (n2 - 1 - p2) * (p2 > 0))
            totals[k // BATCH] += count
        for n, count in enumerate(totals):
            block = xg.at[pl.ds(0, count)]
            pltpu.make_async_remote_copy(
                block, block, x_send.at[n], x_recv.at[0, 0], device_id=(rep, tp), device_id_type=MESH
            ).wait_send()

    def consume(k):
        c, part = k // SPLIT, k % SPLIT
        s, h = segment_order[c // per_segment], c % per_segment
        at = pl.ds(h * width, width)
        target = gsend.at[s - 1, at] if s else gr.at[0, at]
        product = lax.dot_general(
            xg[pl.ds(k * peers, peers)].reshape(peers * tokens, width), cot[part],
            (((0,), (0,)), ((), ())), preferred_element_type=jnp.float32,
        )
        target[...] = target[...] + product if part else product
        if s and part == SPLIT - 1:
            copy = pltpu.make_async_remote_copy(
                gsend.at[s - 1, at], gr.at[s, at], g_send, g_recv.at[h],
                device_id=(rep ^ s, tp), device_id_type=MESH,
            )
            copy.start()

    pairs = [(s, t) for s in range(replicas) for t in range(s, replicas)]
    fold = gr.shape[2] // LANES

    def inner_products(h, sums, chosen, fresh=True):
        if fresh:
            piece = gr.at[pl.ds(0, replicas - 1), pl.ds(h * width, width)]
            pltpu.make_async_copy(piece, piece, g_recv.at[h]).wait()

        def products(n, sums):
            at = pl.ds(pl.multiple_of(h * width + n * SUBLANES, SUBLANES), SUBLANES)
            block = {s: gr[s, at, :] for s in sorted({m for pair in chosen for m in pair})}
            out = []
            for total, (s, t) in zip(sums, pairs):
                if (s, t) not in chosen:
                    out.append(total)
                    continue
                prod = block[s] * block[t]
                part = prod[:, :LANES]
                for f in range(1, fold):
                    part = part + prod[:, f * LANES : (f + 1) * LANES]
                out.append(total + part)
            return tuple(out)

        return lax.fori_loop(0, width // SUBLANES, products, sums)

    sums = tuple(jnp.zeros((SUBLANES, LANES), jnp.float32) for _ in pairs)
    loaded = False
    for kind, k, t in timeline(units, outer, inner):
        if kind == "own":
            own(k)
        elif kind == "line":
            line(k, t)
        elif kind == "cross":
            second_line(k, t, False)
        elif kind == "turn":
            turn(k)
        elif kind == "pass":
            pass_on(k, t, False)
        else:
            if not loaded:
                pltpu.make_async_copy(cot, cot, load_g).wait()
                loaded = True
            for u in range(1, route(k)[1]):
                second_line(k, u, True)
            if k in mixed:
                for u in range(1, outer):
                    pass_on(k, u, True)
            consume(k)
            if k == units - SPLIT - 1:
                for h in range(per_segment - 1):
                    sums = inner_products(h, sums, pairs)
                sums = inner_products(per_segment - 1, sums, [pair for pair in pairs if pair[0]])
    sums = inner_products(per_segment - 1, sums, [pair for pair in pairs if not pair[0]], False)
    lane = lax.broadcasted_iota(jnp.int32, (1, LANES), 1)
    packed = jnp.zeros((1, LANES), jnp.float32)
    for n, total in enumerate(sums):
        packed = jnp.where(lane == n, jnp.sum(total, keepdims=True), packed)
    tile_tp[0] = packed
    for d in range(peers - 1, -1, -1):
        for s in range(replicas - 1, -1, -1):
            if d or s:
                pltpu.make_async_remote_copy(
                    tile_tp.at[0], tile_tp.at[s * peers + d], t_send, t_recv,
                    device_id=(rep ^ s, tp ^ d), device_id_type=MESH,
                ).start()
    pltpu.make_async_copy(states, states, load_s).wait()
    others = tile_tp.at[pl.ds(1, replicas * peers - 1)]
    pltpu.make_async_copy(others, others, t_recv).wait()
    index = {pair: n for n, pair in enumerate(pairs)}
    seen = []
    for s in range(replicas):
        seen.append(jnp.sum(tile_tp[pl.ds(s * peers, peers)], axis=0))
    gram = {}
    for s, t in pairs:
        value = None
        for d in range(replicas):
            p, q = s ^ d, t ^ d
            picked = jnp.where(lane == index[min(p, q), max(p, q)], seen[d], 0.0)
            value = picked if value is None else value + picked
        gram[s, t] = jnp.sum(value, keepdims=True)
    coef = adasum_weights(gram, replicas)
    coef = [jnp.broadcast_to(coef[s], (SUBLANES, gr.shape[2])) for s in range(replicas)]

    masks = []
    mask = replicas // 2
    while mask:
        masks.append(mask)
        mask //= 2
    piece = rows // PIECES

    def w_at(s, q):
        return w_out.at[pl.ds(pl.multiple_of((rep ^ s) * rows + q * piece, piece), piece)]

    last = len(masks) - 1

    def w_send_start(step, s, q):
        m = masks[step]
        pltpu.make_async_remote_copy(
            w_at(s, q), w_at(s, q), w_send, w_last if step == last else w_recv.at[(s ^ m) // 2, q],
            device_id=(rep ^ m, tp), device_id_type=MESH,
        ).start()

    for q in range(PIECES):
        def update(n, carry):
            at = pl.ds(pl.multiple_of(q * piece + n * SUBLANES * 2, SUBLANES * 2), SUBLANES * 2)
            value = None
            for s in range(replicas):
                term = coef[s][:1] * gr[s, at, :]
                value = term if value is None else value + term
            moment_new = BETA_ONE * states[1, at, :] + (1.0 - BETA_ONE) * value
            second_new = BETA_TWO * states[2, at, :] + (1.0 - BETA_TWO) * value * value
            master_new = states[0, at, :] - LEARN * (moment_new / CORRECT_ONE) / (
                jnp.sqrt(second_new / CORRECT_TWO) + 1e-08
            )
            comb[at, :] = value
            mom[at, :] = moment_new
            sec[at, :] = second_new
            mas[at, :] = master_new
            own_at = pl.ds(pl.multiple_of(rep * rows + q * piece + n * SUBLANES * 2, SUBLANES * 2), SUBLANES * 2)
            w_out[own_at, :] = master_new.astype(jnp.bfloat16)
            return carry

        lax.fori_loop(0, piece // (SUBLANES * 2), update, 0)
        for step in range(len(masks)):
            w_send_start(step, 0, q)
    def relay(q, step, s):
        pltpu.make_async_copy(w_at(s, q), w_at(s, q), w_recv.at[s // 2, q]).wait()
        for later in range(step + 1, len(masks)):
            w_send_start(later, s, q)

    held = [0]
    for step, m in enumerate(masks[:-1]):
        fresh = [s ^ m for s in held]
        for q in range(PIECES):
            for s in fresh:
                relay(q, step, s)
        held = held + fresh

    half = w_out.at[pl.ds(0, replicas // 2 * rows)]
    pltpu.make_async_copy(half, half, w_last).wait()
    for at_i in range(outer):
        for at_j in range(inner):
            pl.when((i == at_i) & (j == at_j))(functools.partial(drain, at_i, at_j))
    pltpu.make_async_copy(gsend, gsend, g_send).wait()
    pltpu.make_async_copy(others, others, t_send).wait()
    sent = w_out.at[pl.ds(0, (replicas - 1) * rows)]
    pltpu.make_async_copy(sent, sent, w_send).wait()


def deliver(*refs):
    sources, targets, sem = refs[:5], refs[5:10], refs[10]
    for n, (src, dst) in enumerate(zip(sources, targets)):
        step = src.shape[0] // PIECES
        for q in range(PIECES):
            at = pl.ds(q * step, step)
            pltpu.make_async_copy(src.at[at], dst.at[at], sem.at[n]).start()
    for n, (src, dst) in enumerate(zip(sources, targets)):
        pltpu.make_async_copy(src, dst, sem.at[n]).wait()


def per_device(inputs, cotangent, master, moment, second):
    replicas = lax.axis_size("rep")
    peers = lax.axis_size("tp")
    inner = 1 << (peers.bit_length() - 1) // 2
    outer = peers // inner
    tokens, depth = inputs.shape
    features = cotangent.shape[1]
    rows = depth // replicas
    width = min(LANES, rows)
    chunks = depth // width
    per_segment = rows // width
    units = chunks * SPLIT
    anywhere = pl.BlockSpec(memory_space=pl.ANY)
    vmem = pl.BlockSpec(memory_space=pltpu.VMEM)
    dma = pltpu.SemaphoreType.DMA
    small = pltpu.VMEM((rows, features), jnp.float32)
    results = pl.pallas_call(
        functools.partial(kernel, replicas, outer, inner),
        out_shape=(small, small, small, small, pltpu.VMEM((depth, features), jnp.bfloat16)),
        in_specs=[anywhere] * 5,
        out_specs=(vmem,) * 5,
        scratch_shapes=[
            pltpu.VMEM((units * peers, tokens // SPLIT, width), jnp.bfloat16),
            pltpu.VMEM((SPLIT, cotangent.shape[0] // SPLIT, features), jnp.bfloat16),
            pltpu.VMEM((replicas - 1, rows, features), jnp.float32),
            pltpu.VMEM((replicas, rows, features), jnp.float32),
            pltpu.VMEM((3, rows, features), jnp.float32),
            pltpu.VMEM((replicas * peers, 1, LANES), jnp.float32),
            dma((-(-units // GROUP),)),
            dma(()),
            dma(()),
            dma((-(-units // BATCH),)),
            dma((units, outer + inner - 2)),
            dma((len(MIXED), outer + 1)),
            dma(()),
            dma((per_segment,)),
            dma(()),
            dma(()),
            dma(()),
            dma((replicas // 2, PIECES)),
            dma(()),
        ],
        compiler_params=pltpu.CompilerParams(
            collective_id=0, has_side_effects=True, vmem_limit_bytes=48 * 1024 * 1024
        ),
        name="adasum_adam",
    )(inputs, cotangent, master, moment, second)
    results = [pltpu.with_memory_space_constraint(r, pltpu.VMEM) for r in results]
    return pl.pallas_call(
        deliver,
        out_shape=tuple(jax.ShapeDtypeStruct(r.shape, r.dtype) for r in results),
        in_specs=[vmem] * 5,
        out_specs=(anywhere,) * 5,
        scratch_shapes=[dma((5,))],
        compiler_params=pltpu.CompilerParams(vmem_limit_bytes=1024 * 1024),
        name="deliver",
    )(*results)


def solution(mesh):
    return jax.shard_map(
        per_device,
        mesh=mesh,
        in_specs=(
            P(("rep", "tp"), None),
            P("rep", "tp"),
            P("rep", "tp"),
            P("rep", "tp"),
            P("rep", "tp"),
        ),
        out_specs=(P("rep", "tp"), P("rep", "tp"), P("rep", "tp"), P("rep", "tp"), P(None, "tp")),
        check_vma=False,
    )
```
